128 devices in a mesh: leaf: 32 (over y, x, core), sub: 4 (over z).
Axes of the slice: x: 4, y: 4, z: 4, core: 2. Of those that a mesh axis runs over, the one named last changes fastest.
Arguments:
- charges: float32 [16, 64, 4, 32, 2048], P(None, None, 'sub', 'leaf'), may hold values from -6 to 6
- ordering: int32 [4, 32, 2048], P('sub', 'leaf'), may hold values from 0 to 2047, each once within a row
- jitter: float32 [3, 4, 32, 2048], P(None, 'sub', 'leaf'), may hold values from 0 to 1
- leaf_bases: float32 [4, 32, 64, 2048], P('sub', 'leaf'), may hold values from -0.125 to 0.125
- transfer: float32 [7, 2, 64, 64], replicated, may hold values from -0.5 to 0.5
- coupling: float32 [7, 2, 64, 64], replicated, may hold values from -0.75 to 0.75
Outputs:
- potential: float32 [16, 64, 4, 32, 2048], P(None, None, 'sub', 'leaf')
The draws below stay inside these ranges and needn't reach their ends.
All inputs are finite; a program needn't handle non-finite values.
Results may differ from the reference program's by a relative error of at most 0.0003.
Values sent between devices are 32-bit elements; how exact they have to be, the bound alone decides.
A program may use at most 128 MiB of HBM per device.

```python
import jax
import jax.numpy as jnp
from jax import lax

VEC = 64
RANK = 64
PTS = 2048
SETS = 16
STRIP = 512
CLUSTERS = 32
SUBTREES = 4
LEVELS = 7


def shard_levels(own_key, shape, shards, smallest, largest):
    gain = 1.0
    for position, parts in shards:
        steps = jax.random.uniform(jax.random.fold_in(jax.random.fold_in(own_key, 6), position), (parts,), jnp.float32, smallest / len(shards), largest / len(shards))
        gain = gain * jnp.repeat(jnp.exp(steps), shape[position] // parts).reshape((-1,) + (1,) * (len(shape) - 1 - position))
    return gain


def scatter_about(rng, dims, width, limit, pieces=(), held_as=jnp.bfloat16):
    entries = jax.random.normal(rng, dims, jnp.float32) * width
    if len(pieces) > 0:
        entries = shard_levels(rng, dims, pieces, -0.22, 0.18) * entries
    return jnp.clip(entries, min=-limit, max=limit).astype(held_as)


def setup_inputs(seed: int = 0) -> dict:
    key_list = jax.random.split(jax.random.key(seed), 7)
    charges = scatter_about(key_list[0], (SETS, VEC, SUBTREES, CLUSTERS, PTS), 1.0, 6.0, ((2, 4), (3, 32)), jnp.float32)
    ordering = jax.vmap(lambda own: jax.random.permutation(own, PTS))(jax.random.split(key_list[1], SUBTREES * CLUSTERS)).reshape((SUBTREES, CLUSTERS, PTS)).astype(jnp.int32)
    jitter = jnp.clip(1.0 * jax.random.uniform(key_list[2], (3, SUBTREES, CLUSTERS, PTS), jnp.float32) ** shard_levels(key_list[2], (3, SUBTREES, CLUSTERS, PTS), ((1, 4), (2, 32)), -0.2, 0.2), 0.0, 1.0)
    leaf_bases = scatter_about(key_list[3], (SUBTREES, CLUSTERS, RANK, PTS), PTS ** -0.5, 0.125, ((0, 4), (1, 32)), jnp.float32)
    transfer = scatter_about(key_list[4], (LEVELS, 2, RANK, RANK), (2 * RANK) ** -0.5, 0.5, (), jnp.float32)
    coupling = scatter_about(key_list[5], (LEVELS, 2, RANK, RANK), RANK ** -0.5, 0.75, (), jnp.float32)
    return dict(charges=charges, ordering=ordering, jitter=jitter, leaf_bases=leaf_bases, transfer=transfer, coupling=coupling)


DELTA_SQ = 0.0025
PRECISE = lax.Precision.HIGHEST

def near_field(src_charges, src_places, tgt_places, near_scale):
    count = tgt_places.shape[1]
    block_rows = min(count, 512)

    def accumulate(step, result):
        first_row = (step * block_rows).astype(jnp.int32)
        targets = lax.dynamic_slice_in_dim(tgt_places, first_row, block_rows, 1)
        distance = jnp.zeros((src_places.shape[1], block_rows), jnp.float32)
        for component in range(3):
            spacing = src_places[component][:, None] - targets[component][None, :]
            distance = distance + spacing * spacing
        weight = near_scale * lax.rsqrt(distance + DELTA_SQ)
        product = jnp.dot(src_charges, weight, precision=PRECISE, preferred_element_type=jnp.float32)
        return lax.dynamic_update_slice_in_dim(result, product, first_row, 1)
    start_value = jnp.zeros((src_charges.shape[0], count), jnp.float32)
    return lax.fori_loop(0, count // block_rows, accumulate, start_value)

def pick_order(block_data, indices):
    return jnp.take(block_data, indices, axis=1)

def reference(charges, ordering, jitter, leaf_bases, transfer, coupling):
    set_count, vector_count = (charges.shape[0], charges.shape[1])
    row_count = set_count * vector_count
    clusters_all = SUBTREES * CLUSTERS
    grouped = charges.reshape(row_count, SUBTREES, CLUSTERS, PTS).transpose(1, 2, 0, 3)
    tree_charges = jax.vmap(jax.vmap(pick_order))(grouped, ordering)
    cluster_ids = jnp.arange(CLUSTERS, dtype=jnp.float32)[None, :, None]
    point_ids = jnp.arange(PTS, dtype=jnp.float32)[None, None, :]
    along_axis = cluster_ids + (point_ids + jitter[0]) / PTS
    places = jnp.stack([along_axis, jitter[1], jitter[2]], axis=2)
    sources = jnp.concatenate([tree_charges, places], axis=2)
    padded = jnp.pad(sources, ((0, 0), (1, 1), (0, 0), (0, 0)))
    near_scale = PTS ** (-0.5)

    def near_one(flat_index):
        sub_index = (flat_index // CLUSTERS).astype(jnp.int32)
        leaf_index = (flat_index % CLUSTERS).astype(jnp.int32)
        zero_index = jnp.zeros((), jnp.int32)
        window = lax.dynamic_slice(padded, (sub_index, leaf_index, zero_index, zero_index), (1, 3, row_count + 3, PTS))[0]
        joined = jnp.concatenate([window[0, :, PTS - STRIP:], window[1], window[2, :, :STRIP]], axis=1)
        return near_field(joined[:row_count], joined[row_count:], window[1, row_count:], near_scale)
    near_all = lax.map(near_one, jnp.arange(clusters_all, dtype=jnp.int32))
    flat_tree = tree_charges.reshape(clusters_all, row_count, PTS)
    flat_bases = leaf_bases.reshape(clusters_all, RANK, PTS)
    moment = jnp.einsum('gsp,grp->gsr', flat_tree, flat_bases, precision=PRECISE)
    moments = [moment]
    for level_index in range(LEVELS):
        current = moments[-1]
        parent = jnp.einsum('nsa,ab->nsb', current[0::2], transfer[level_index, 0], precision=PRECISE)
        parent = parent + jnp.einsum('nsa,ab->nsb', current[1::2], transfer[level_index, 1], precision=PRECISE)
        moments.append(parent)
    expansion = jnp.zeros((1, row_count, RANK), jnp.float32)
    for level_index in reversed(range(LEVELS)):
        current = moments[level_index]
        count = current.shape[0]
        sibling = current.reshape(count // 2, 2, row_count, RANK)[:, ::-1].reshape(count, row_count, RANK)
        inherited = jnp.repeat(expansion, 2, axis=0)
        branch_bits = jnp.arange(count, dtype=jnp.int32) % 2
        couple_mats = coupling[level_index][branch_bits]
        transfer_mats = transfer[level_index][branch_bits]
        expansion = jnp.einsum('nsa,nra->nsr', sibling, couple_mats, precision=PRECISE) + jnp.einsum('nsa,nra->nsr', inherited, transfer_mats, precision=PRECISE)
    far_all = jnp.einsum('gsr,grp->gsp', expansion, flat_bases, precision=PRECISE)
    potential = near_all + far_all
    potential = potential.reshape(SUBTREES, CLUSTERS, set_count, vector_count, PTS).transpose(2, 3, 0, 1, 4)
    return potential
```

```python
import jax
import jax.numpy as jnp
from jax import lax
from jax.experimental import pallas as pl
from jax.experimental.pallas import tpu as pltpu
from jax.sharding import PartitionSpec as P

DELTA_SQ = 0.0025
PRECISE = lax.Precision.HIGHEST
F8 = jnp.float8_e4m3fn
BF = jnp.bfloat16
F32 = jnp.float32
GAIN = 16.0
TOP = 384.0
FEATS = 32
SUB = 256
LIMIT = 60 * 1024 * 1024


def swapped(value, axis, stride):
    mask = 2**stride
    pairs = [(source, source ^ mask) for source in range(lax.axis_size(axis))]
    return lax.ppermute(value, axis, pairs)


def lift_pair(current, sibling, branch_bit, transfer_pair):
    left_part = jnp.where(branch_bit == 0, current, sibling)
    right_part = jnp.where(branch_bit == 0, sibling, current)
    parent = jnp.dot(
        left_part, transfer_pair[0], precision=PRECISE, preferred_element_type=jnp.float32
    )
    return parent + jnp.dot(
        right_part, transfer_pair[1], precision=PRECISE, preferred_element_type=jnp.float32
    )


def contract_last(left_mat, right_mat):
    return lax.dot_general(
        left_mat,
        right_mat,
        (((1,), (1,)), ((), ())),
        precision=PRECISE,
        preferred_element_type=jnp.float32,
    )


def mm(left, right):
    return jnp.dot(left, right, preferred_element_type=F32)


def mm_nt(left, right):
    return lax.dot_general(left, right, (((1,), (1,)), ((), ())), preferred_element_type=F32)


def rounded(value):
    return lax.reduce_precision(value, 8, 7)


def pieces(value):
    high = rounded(value)
    middle = rounded(value - high)
    return high, middle, rounded(value - high - middle)


def features(coords):
    parts = [pieces(coords[axis]) for axis in range(3)]
    norm = jnp.sum(coords * coords, axis=0)
    ones = jnp.ones_like(norm)
    source = []
    target = []
    for part in parts:
        for left, right in ((0, 0), (0, 1), (1, 0), (1, 1), (0, 2), (2, 0)):
            source.append(part[left])
            target.append(-2.0 * part[right])
    softened = norm + DELTA_SQ / (GAIN * GAIN)
    source += list(pieces(softened)) + [ones] * 3
    target += [ones] * 3 + list(pieces(norm))
    blank = [jnp.zeros_like(norm)] * (FEATS - len(source))
    return jnp.stack(source + blank).astype(BF), jnp.stack(target + blank).astype(BF)


def scaled(rows):
    top = jnp.maximum(jnp.max(jnp.abs(rows), axis=1, keepdims=True), 1e-30)
    full = rows * (TOP / top)
    high = full.astype(BF)
    return full, high, full - high.astype(F32), top * (1.0 / TOP)


def prepare_kernel(
    q_ref, order_ref, x_ref, qh_ref, q8h_ref, q8l_ref, unit_ref, tail_ref, head_ref, moment_ref,
    feat_ref, pick, pick8, basis,
):
    points = q_ref.shape[1]
    strip = tail_ref.shape[1]
    rank = moment_ref.shape[1]

    @pl.when(pl.program_id(0) == 0)
    def _():
        @pl.loop(0, points // SUB)
        def _(step):
            rows = pl.ds(pl.multiple_of(step * SUB, SUB), SUB)
            own = lax.broadcasted_iota(jnp.int32, (SUB, strip), 0) + step * SUB
            for part in range(points // strip):
                columns = slice(part * strip, (part + 1) * strip)
                hit = jnp.where(own == order_ref[:, columns], 1.0, 0.0)
                pick[rows, columns] = hit.astype(BF)
                if part == 0:
                    pick8[rows, :strip] = hit.astype(F8)
                if part == points // strip - 1:
                    pick8[rows, strip:] = hit.astype(F8)
            moved = mm_nt(pick[rows, :], x_ref[...]).astype(BF)
            feat_ref[rows, :] = moved[:, 2 * rank :]
            basis[rows, :] = moved[:, : 2 * rank]

    full, high, rest, unit = scaled(q_ref[...])
    low8 = rest.astype(F8)
    qh_ref[...] = high
    q8h_ref[...] = full.astype(F8)
    q8l_ref[...] = low8
    unit_ref[...] = jnp.broadcast_to(unit, unit_ref.shape)
    head_ref[...] = (mm(high, pick[:, :strip]) + mm(low8, pick8[:, :strip])) * unit
    last = points - strip
    tail_ref[...] = (mm(high, pick[:, last:]) + mm(low8, pick8[:, strip:])) * unit
    both = mm(high, basis[...])
    moment_ref[...] = (
        both[:, :rank] + both[:, rank:] + mm(rest.astype(BF), basis[:, :rank])
    ) * unit


def prepare(charges, order, stacked):
    rows, points = charges.shape
    strip = points // 4
    rank = (stacked.shape[0] - FEATS) // 2
    chunk = 256
    whole = lambda shape: pl.BlockSpec(shape, lambda step: (0, 0))
    sliced = lambda width: pl.BlockSpec((chunk, width), lambda step: (step, 0))
    shape = jax.ShapeDtypeStruct
    return pl.pallas_call(
        prepare_kernel,
        grid=(rows // chunk,),
        in_specs=[sliced(points), whole(order.shape), whole(stacked.shape)],
        out_specs=[sliced(points)] * 3
        + [sliced(128), sliced(strip), sliced(strip), sliced(rank), whole((points, FEATS))],
        out_shape=[
            shape((rows, points), BF),
            shape((rows, points), F8),
            shape((rows, points), F8),
            shape((rows, 128), F32),
            shape((rows, strip), F32),
            shape((rows, strip), F32),
            shape((rows, rank), F32),
            shape((points, FEATS), BF),
        ],
        scratch_shapes=[
            pltpu.VMEM((points, points), BF),
            pltpu.VMEM((points, 2 * strip), F8),
            pltpu.VMEM((points, 2 * rank), BF),
        ],
        compiler_params=pltpu.CompilerParams(vmem_limit_bytes=LIMIT),
        cost_estimate=pl.CostEstimate(
            flops=14_000_000_000, bytes_accessed=28_000_000, transcendentals=0
        ),
        name="prepare",
    )(charges, order, stacked)


def weigh(source_ref, target, first, last, slot, w, w8h, w8l):
    for row in range(first, last, 128):
        rows = slice(row, row + 128)
        weight = lax.rsqrt(mm(source_ref[rows, :], target))
        high = weight.astype(BF)
        w[slot, rows, :] = high
        w8h[slot, rows, :] = weight.astype(F8)
        w8l[slot, rows, :] = (weight - high.astype(F32)).astype(F8)


def sweep(source_ref, target_ref, row_count, w, w8h, w8l, emit):
    points = source_ref.shape[0]
    blocks = target_ref.shape[1] // SUB
    step = pl.program_id(0)
    parts = 4

    def target(block):
        return target_ref[:, pl.ds(pl.multiple_of(block * SUB, SUB), SUB)]

    @pl.when(step == 0)
    def _():
        weigh(source_ref, target(0), 0, points, 0, w, w8h, w8l)

    for slot in range(2):
        coming = target(jnp.minimum(2 * step + slot + 1, blocks - 1))
        for part in range(parts):
            count = row_count // parts
            weigh(
                source_ref,
                coming,
                part * points // parts,
                (part + 1) * points // parts,
                1 - slot,
                w,
                w8h,
                w8l,
            )
            emit(slice(part * count, (part + 1) * count), slot)


def own_kernel(qh_ref, q8h_ref, q8l_ref, unit_ref, source_ref, target_ref, out_ref, w, w8h, w8l):
    def emit(rows, slot):
        total = mm(qh_ref[rows, :], w[slot])
        total = total + mm(q8h_ref[rows, :], w8l[slot])
        total = total + mm(q8l_ref[rows, :], w8h[slot])
        out_ref[rows, slot * SUB : (slot + 1) * SUB] = total * unit_ref[rows, 0:1]

    sweep(source_ref, target_ref, out_ref.shape[0], w, w8h, w8l, emit)


def weight_scratch(count):
    return [
        pltpu.VMEM((2, count, SUB), BF),
        pltpu.VMEM((2, count, SUB), F8),
        pltpu.VMEM((2, count, SUB), F8),
    ]


def own_near(high, high8, low8, unit, source, target):
    rows, points = high.shape
    whole = lambda a: pl.BlockSpec(a.shape, lambda step: (0, 0), pipeline_mode=pl.Buffered(1))
    return pl.pallas_call(
        own_kernel,
        grid=(points // (2 * SUB),),
        in_specs=[whole(a) for a in (high, high8, low8, unit, source, target)],
        out_specs=pl.BlockSpec((rows, 2 * SUB), lambda step: (0, step)),
        out_shape=jax.ShapeDtypeStruct((rows, points), F32),
        scratch_shapes=weight_scratch(points),
        compiler_params=pltpu.CompilerParams(vmem_limit_bytes=LIMIT),
        cost_estimate=pl.CostEstimate(
            flops=17_000_000_000, bytes_accessed=16_000_000, transcendentals=4_000_000
        ),
        name="own_near",
    )(high, high8, low8, unit, source, target)


def rest_kernel(
    factor, left_ref, right_ref, source_ref, target_ref, expansion_ref, basis_ref, near_ref,
    out_ref, qh, q8h, q8l, units, far, w, w8h, w8l,
):
    strip = left_ref.shape[1]
    rank = expansion_ref.shape[1]
    row_count = out_ref.shape[0]

    @pl.when(pl.program_id(0) == 0)
    def _():
        @pl.loop(0, row_count // SUB)
        def _(step):
            rows = pl.ds(pl.multiple_of(step * SUB, SUB), SUB)
            joined = jnp.concatenate([left_ref[rows, :], right_ref[rows, :]], axis=1)
            full, high, rest, unit = scaled(joined)
            qh[rows, :] = high
            q8h[rows, :] = full.astype(F8)
            q8l[rows, :] = rest.astype(F8)
            units[rows, :] = jnp.broadcast_to(unit, (SUB, units.shape[1]))
            value = expansion_ref[rows, :]
            top = value.astype(BF)
            low = (value - top.astype(F32)).astype(BF)
            far[rows, :rank] = top
            far[rows, rank : 2 * rank] = low
            far[rows, 2 * rank :] = top

    def emit(rows, slot):
        columns = slice(slot * SUB, (slot + 1) * SUB)
        total = mm(qh[rows, :], w[slot])
        total = total + mm(q8h[rows, :], w8l[slot])
        total = total + mm(q8l[rows, :], w8h[slot])
        total = total * units[rows, 0:1] + near_ref[rows, columns]
        out_ref[rows, columns] = total * factor + mm(far[rows, :], basis_ref[:, columns])

    sweep(source_ref, target_ref, row_count, w, w8h, w8l, emit)


def finish(left, right, source, target, expansion, basis, near, factor):
    rows, points = near.shape
    strip = left.shape[1]
    whole = lambda a: pl.BlockSpec(a.shape, lambda step: (0, 0), pipeline_mode=pl.Buffered(1))
    block = lambda count: pl.BlockSpec((count, 2 * SUB), lambda step: (0, step))
    return pl.pallas_call(
        lambda *refs: rest_kernel(factor, *refs),
        grid=(points // (2 * SUB),),
        in_specs=[whole(a) for a in (left, right, source, target, expansion)]
        + [block(basis.shape[0]), block(rows)],
        out_specs=block(rows),
        out_shape=jax.ShapeDtypeStruct((rows, points), F32),
        scratch_shapes=[
            pltpu.VMEM((rows, 2 * strip), BF),
            pltpu.VMEM((rows, 2 * strip), F8),
            pltpu.VMEM((rows, 2 * strip), F8),
            pltpu.VMEM((rows, 128), F32),
            pltpu.VMEM((rows, basis.shape[0]), BF),
        ]
        + weight_scratch(2 * strip),
        compiler_params=pltpu.CompilerParams(vmem_limit_bytes=LIMIT),
        cost_estimate=pl.CostEstimate(
            flops=10_000_000_000, bytes_accessed=21_000_000, transcendentals=2_000_000
        ),
        name="finish",
    )(left, right, source, target, expansion, basis, near)


def body(charges, ordering, jitter, leaf_bases, transfer, coupling):
    set_count, vector_count = (charges.shape[0], charges.shape[1])
    points = charges.shape[4]
    strip_width = points // 4
    row_count = set_count * vector_count
    near_scale = points ** (-0.5)
    flattened = charges.reshape(row_count, points)
    offsets = jitter.reshape(3, points)
    indices = jnp.arange(points, dtype=jnp.float32)
    places = jnp.stack([(indices + offsets[0]) / points, offsets[1], offsets[2]])
    places = (places - 0.5) / GAIN
    leaf_basis = leaf_bases.reshape(leaf_bases.shape[2], points)
    basis_top = rounded(leaf_basis)
    basis_low = rounded(leaf_basis - basis_top)
    source_rows, target_rows = features(places)
    stacked = jnp.concatenate([basis_top.astype(BF), basis_low.astype(BF), source_rows])
    high, high8, low8, unit, tail, head, moment, own_source = prepare(
        flattened, ordering.reshape(1, points), stacked
    )
    count = lax.axis_size("leaf")
    onward = [(i, i + 1) for i in range(count - 1)]
    back = [(i + 1, i) for i in range(count - 1)]
    left = lax.ppermute(tail, "leaf", onward)
    right = lax.ppermute(head, "leaf", back)
    left_places = lax.ppermute(places[:, points - strip_width :], "leaf", onward)
    right_places = lax.ppermute(places[:, :strip_width], "leaf", back)
    side = jnp.array([[1.0 / GAIN], [0.0], [0.0]], F32)
    strip_places = jnp.concatenate([left_places - side, right_places + side], axis=1)
    strip_source = features(strip_places)[0].T
    near_part = own_near(high, high8, low8, unit, own_source, target_rows)
    leaf_levels = lax.axis_size("leaf").bit_length() - 1
    sub_levels = lax.axis_size("sub").bit_length() - 1
    position = lax.axis_index("leaf")
    siblings = []
    branch_bits = []
    current = moment
    for bit_index in range(leaf_levels):
        sibling = swapped(current, "leaf", bit_index)
        branch_bit = position >> bit_index & 1
        current = lift_pair(current, sibling, branch_bit, transfer[bit_index])
        siblings.append(sibling)
        branch_bits.append(branch_bit)
    sub_position = lax.axis_index("sub")
    for bit_index in range(sub_levels):
        level_index = leaf_levels + bit_index
        sibling = swapped(current, "sub", bit_index)
        branch_bit = sub_position >> bit_index & 1
        current = lift_pair(current, sibling, branch_bit, transfer[level_index])
        siblings.append(sibling)
        branch_bits.append(branch_bit)
    expansion = jnp.zeros((row_count, moment.shape[1]), jnp.float32)
    for level_index in reversed(range(leaf_levels + sub_levels)):
        couple_mat = lax.dynamic_index_in_dim(
            coupling[level_index], branch_bits[level_index], 0, keepdims=False
        )
        transfer_mat = lax.dynamic_index_in_dim(
            transfer[level_index], branch_bits[level_index], 0, keepdims=False
        )
        expansion = contract_last(siblings[level_index], couple_mat) + contract_last(
            expansion, transfer_mat
        )
    basis_rows = jnp.concatenate([basis_top, basis_top, basis_low]).astype(BF)
    potential = finish(
        left,
        right,
        strip_source,
        target_rows,
        expansion,
        basis_rows,
        near_part,
        near_scale / GAIN,
    )
    return potential.reshape(set_count, vector_count, 1, 1, points)


def solution(mesh):
    in_specs = (
        P(None, None, "sub", "leaf", None),
        P("sub", "leaf", None),
        P(None, "sub", "leaf", None),
        P("sub", "leaf", None, None),
        P(),
        P(),
    )
    out_specs = P(None, None, "sub", "leaf", None)
    return jax.shard_map(body, mesh=mesh, in_specs=in_specs, out_specs=out_specs, check_vma=False)
```

```python
import jax
import jax.numpy as jnp
from jax import lax
from jax.experimental import pallas as pl
from jax.experimental.pallas import tpu as pltpu
from jax.sharding import PartitionSpec as P

DELTA_SQ = 0.0025
PRECISE = lax.Precision.HIGHEST
F8 = jnp.float8_e4m3fn
BF = jnp.bfloat16
F32 = jnp.float32
GAIN = 16.0
TOP = 384.0
FEATS = 32
SUB = 256
OUT_BLOCKS = 4
LANES = 128
PAD = 8
LIMIT = 60 * 1024 * 1024


def swapped(value, axis, stride):
    mask = 2**stride
    pairs = [(source, source ^ mask) for source in range(lax.axis_size(axis))]
    return lax.ppermute(value, axis, pairs)


def lift_pair(current, sibling, branch_bit, transfer_pair):
    left_part = jnp.where(branch_bit == 0, current, sibling)
    right_part = jnp.where(branch_bit == 0, sibling, current)
    parent = jnp.dot(
        left_part, transfer_pair[0], precision=PRECISE, preferred_element_type=jnp.float32
    )
    return parent + jnp.dot(
        right_part, transfer_pair[1], precision=PRECISE, preferred_element_type=jnp.float32
    )


def contract_last(left_mat, right_mat):
    return lax.dot_general(
        left_mat,
        right_mat,
        (((1,), (1,)), ((), ())),
        precision=PRECISE,
        preferred_element_type=jnp.float32,
    )


def mm(left, right):
    return jnp.dot(left, right, preferred_element_type=F32)


def mm_nt(left, right):
    return lax.dot_general(left, right, (((1,), (1,)), ((), ())), preferred_element_type=F32)


def split(value):
    high = value.astype(BF)
    return high, value - high.astype(F32)


def features(coords, source_ref, target_ref, columns):
    ones = jnp.ones_like(coords[0])
    norm = sum(coord * coord for coord in coords)

    def pieces(value):
        out = []
        for _ in range(3):
            high, value = split(value)
            out.append(high.astype(F32))
        return out

    source = []
    target = []
    for coord in coords:
        part = pieces(coord)
        for left, right in ((0, 0), (0, 1), (1, 0), (1, 1), (0, 2), (2, 0)):
            source.append(part[left])
            target.append(-2.0 * part[right])
    source += pieces(norm + DELTA_SQ / (GAIN * GAIN)) + [ones] * 3
    target += [ones] * 3 + pieces(norm)
    blank = [jnp.zeros_like(norm)] * (FEATS - len(source))
    for ref, rows in ((source_ref, source + blank), (target_ref, target + blank)):
        if ref is not None:
            for index, row in enumerate(rows):
                ref[index : index + 1, columns] = row


def scaled(rows):
    top = jnp.maximum(jnp.max(jnp.abs(rows), axis=1, keepdims=True), 1e-30)
    full = rows * (TOP / top)
    high = full.astype(BF)
    return full, high, full - high.astype(F32), top * (1.0 / TOP)


def prepare_kernel(
    q_ref, order_ref, jitter_ref, bases_ref,
    qh_ref, q8h_ref, q8l_ref, unit_ref, tail_ref, head_ref, moment_ref, feat_ref, target_ref,
    pick, pick8, basis, moved, source_rows, target_rows,
):
    points = order_ref.shape[1]
    strip = tail_ref.shape[1]
    rank = bases_ref.shape[0]
    chunk = qh_ref.shape[0]
    tiles = points // LANES
    last = points - strip
    now = pl.program_id(0)

    @pl.when(now == 0)
    def _():
        index = lax.broadcasted_iota(jnp.int32, (1, points), 1).astype(F32)
        coords = [(index + jitter_ref[0]) * (1.0 / points), jitter_ref[1], jitter_ref[2]]
        coords = [(coord - 0.5) * (1.0 / GAIN) for coord in coords]
        features(coords, source_rows, target_rows, slice(0, points))
        target_ref[...] = target_rows[...].astype(BF)
        rows = tail_ref.shape[0] - PAD
        for axis in range(3):
            tail_ref[rows + axis : rows + axis + 1, :] = coords[axis][:, last:]
            head_ref[rows + axis : rows + axis + 1, :] = coords[axis][:, :strip]
        blank = jnp.zeros((PAD - 3, strip), F32)
        tail_ref[rows + 3 :, :] = blank
        head_ref[rows + 3 :, :] = blank
        high, low = split(bases_ref[...])
        moved[:rank, :] = high
        moved[rank : 2 * rank, :] = low.astype(BF)
        moved[2 * rank :, :] = source_rows[...].astype(BF)

        @pl.loop(0, points // SUB)
        def _(step):
            rows = pl.ds(pl.multiple_of(step * SUB, SUB), SUB)
            own = lax.broadcasted_iota(jnp.int32, (SUB, strip), 0) + step * SUB
            for part in range(points // strip):
                columns = slice(part * strip, (part + 1) * strip)
                hit = jnp.where(own == order_ref[:, columns], 1.0, 0.0)
                pick[rows, columns] = hit.astype(BF)
                if part == 0:
                    pick8[rows, :strip] = hit.astype(F8)
                if part == points // strip - 1:
                    pick8[rows, strip:] = hit.astype(F8)
            placed = mm_nt(pick[rows, :], moved[...]).astype(BF)
            feat_ref[rows, :] = placed[:, 2 * rank :]
            basis[rows, :] = placed[:, : 2 * rank]

    block = [q_ref[pl.ds(tile, chunk, stride=tiles), :] for tile in range(tiles)]
    full, high, rest, unit = scaled(jnp.concatenate(block, axis=1))
    low8 = rest.astype(F8)
    qh_ref[...] = high
    q8h_ref[...] = full.astype(F8)
    q8l_ref[...] = low8
    unit_ref[...] = jnp.broadcast_to(unit, unit_ref.shape)
    rows = pl.ds(pl.multiple_of(now * chunk, chunk), chunk)
    head_ref[rows, :] = (mm(high, pick[:, :strip]) + mm(low8, pick8[:, :strip])) * unit
    tail_ref[rows, :] = (mm(high, pick[:, last:]) + mm(low8, pick8[:, strip:])) * unit
    both = mm(high, basis[...])
    moment_ref[...] = (
        both[:, :rank] + both[:, rank:] + mm(rest.astype(BF), basis[:, :rank])
    ) * unit


def prepare(charges, order, jitter, bases):
    points = order.shape[1]
    tiles = points // LANES
    rows = charges.shape[0] // tiles
    strip = points // 4
    rank = bases.shape[0]
    chunk = 256
    whole = lambda shape: pl.BlockSpec(shape, lambda step: (0,) * len(shape))
    sliced = lambda width: pl.BlockSpec((chunk, width), lambda step: (step, 0))
    shape = jax.ShapeDtypeStruct
    return pl.pallas_call(
        prepare_kernel,
        grid=(rows // chunk,),
        in_specs=[
            pl.BlockSpec((chunk * tiles, LANES), lambda step: (step, 0)),
            whole(order.shape),
            whole(jitter.shape),
            whole(bases.shape),
        ],
        out_specs=[sliced(points)] * 3
        + [sliced(LANES), whole((rows + PAD, strip)), whole((rows + PAD, strip)), sliced(rank)]
        + [whole((points, FEATS)), whole((FEATS, points))],
        out_shape=[
            shape((rows, points), BF),
            shape((rows, points), F8),
            shape((rows, points), F8),
            shape((rows, LANES), F32),
            shape((rows + PAD, strip), F32),
            shape((rows + PAD, strip), F32),
            shape((rows, rank), F32),
            shape((points, FEATS), BF),
            shape((FEATS, points), BF),
        ],
        scratch_shapes=[
            pltpu.VMEM((points, points), BF),
            pltpu.VMEM((points, 2 * strip), F8),
            pltpu.VMEM((points, 2 * rank), BF),
            pltpu.VMEM((2 * rank + FEATS, points), BF),
            pltpu.VMEM((FEATS, points), F32),
            pltpu.VMEM((FEATS, points), F32),
        ],
        compiler_params=pltpu.CompilerParams(vmem_limit_bytes=LIMIT),
        cost_estimate=pl.CostEstimate(
            flops=14_000_000_000, bytes_accessed=28_000_000, transcendentals=0
        ),
        name="prepare",
    )(charges, order, jitter, bases)


def weigh(source_ref, target, first, last, slot, w, w8h, w8l):
    for row in range(first, last, 128):
        rows = slice(row, row + 128)
        weight = lax.rsqrt(mm(source_ref[rows, :], target))
        high = weight.astype(BF)
        w[slot, rows, :] = high
        w8h[slot, rows, :] = weight.astype(F8)
        w8l[slot, rows, :] = (weight - high.astype(F32)).astype(F8)


def sweep(source_ref, target_ref, row_count, w, w8h, w8l, emit, count):
    points = source_ref.shape[0]
    blocks = target_ref.shape[1] // SUB
    step = pl.program_id(0)
    parts = 4

    def target(block):
        return target_ref[:, pl.ds(pl.multiple_of(block * SUB, SUB), SUB)]

    @pl.when(step == 0)
    def _():
        weigh(source_ref, target(0), 0, points, 0, w, w8h, w8l)

    height = row_count // parts
    for block in range(count):
        slot = block % 2
        coming = target(jnp.minimum(count * step + block + 1, blocks - 1))
        for part in range(parts):
            weigh(
                source_ref,
                coming,
                part * points // parts,
                (part + 1) * points // parts,
                1 - slot,
                w,
                w8h,
                w8l,
            )
            emit(slice(part * height, (part + 1) * height), block, slot)


def own_kernel(qh_ref, q8h_ref, q8l_ref, unit_ref, source_ref, target_ref, out_ref, w, w8h, w8l):
    def emit(rows, block, slot):
        total = mm(qh_ref[rows, :], w[slot])
        total = total + mm(q8h_ref[rows, :], w8l[slot])
        total = total + mm(q8l_ref[rows, :], w8h[slot])
        out_ref[rows, block * SUB : (block + 1) * SUB] = total * unit_ref[rows, 0:1]

    sweep(source_ref, target_ref, out_ref.shape[0], w, w8h, w8l, emit, 2)


def weight_scratch(count):
    return [
        pltpu.VMEM((2, count, SUB), BF),
        pltpu.VMEM((2, count, SUB), F8),
        pltpu.VMEM((2, count, SUB), F8),
    ]


def own_near(high, high8, low8, unit, source, target):
    rows, points = high.shape
    whole = lambda a: pl.BlockSpec(a.shape, lambda step: (0, 0), pipeline_mode=pl.Buffered(1))
    return pl.pallas_call(
        own_kernel,
        grid=(points // (2 * SUB),),
        in_specs=[whole(a) for a in (high, high8, low8, unit, source, target)],
        out_specs=pl.BlockSpec((rows, 2 * SUB), lambda step: (0, step)),
        out_shape=jax.ShapeDtypeStruct((rows, points), F32),
        scratch_shapes=weight_scratch(points),
        compiler_params=pltpu.CompilerParams(vmem_limit_bytes=LIMIT),
        cost_estimate=pl.CostEstimate(
            flops=17_000_000_000, bytes_accessed=16_000_000, transcendentals=4_000_000
        ),
        name="own_near",
    )(high, high8, low8, unit, source, target)


def rest_kernel(
    factor, left_ref, right_ref, target_ref, expansion_ref, bases_ref, near_ref,
    out_ref, qh, q8h, q8l, units, far, basis, source_rows, source, w, w8h, w8l,
):
    strip = left_ref.shape[1]
    rank = expansion_ref.shape[1]
    row_count = near_ref.shape[0]

    @pl.when(pl.program_id(0) == 0)
    def _():
        for ref, shift, columns in (
            (left_ref, -1.0, slice(0, strip)),
            (right_ref, 1.0, slice(strip, 2 * strip)),
        ):
            coords = [ref[row_count + axis : row_count + axis + 1, :] for axis in range(3)]
            coords[0] = coords[0] + shift / GAIN
            features(coords, source_rows, None, columns)
        source[...] = jnp.transpose(source_rows[...]).astype(BF)

        @pl.loop(0, row_count // SUB)
        def _(step):
            rows = pl.ds(pl.multiple_of(step * SUB, SUB), SUB)
            joined = jnp.concatenate([left_ref[rows, :], right_ref[rows, :]], axis=1)
            full, high, rest, unit = scaled(joined)
            qh[rows, :] = high
            q8h[rows, :] = full.astype(F8)
            q8l[rows, :] = rest.astype(F8)
            units[rows, :] = jnp.broadcast_to(unit, (SUB, units.shape[1]))
            top, low = split(expansion_ref[rows, :])
            far[rows, :rank] = top
            far[rows, rank : 2 * rank] = low.astype(BF)
            far[rows, 2 * rank :] = top

        top, low = split(bases_ref[...])
        basis[:rank, :] = top
        basis[rank : 2 * rank, :] = top
        basis[2 * rank :, :] = low.astype(BF)

    def emit(rows, block, slot):
        total = mm(qh[rows, :], w[slot])
        total = total + mm(q8h[rows, :], w8l[slot])
        total = total + mm(q8l[rows, :], w8h[slot])
        inner = slice(block * SUB, (block + 1) * SUB)
        total = total * units[rows, 0:1] + near_ref[rows, inner]
        columns = pl.ds(
            pl.multiple_of((pl.program_id(0) * OUT_BLOCKS + block) * SUB, SUB), SUB
        )
        total = total * factor + mm(far[rows, :], basis[:, columns])
        first = rows.start * PAD
        for part in range(SUB // LANES):
            place = first + block * (SUB // LANES) + part
            out_ref[pl.ds(place, rows.stop - rows.start, stride=PAD), :] = total[
                :, part * LANES : (part + 1) * LANES
            ]

    sweep(source, target_ref, row_count, w, w8h, w8l, emit, OUT_BLOCKS)


def finish(left, right, target, expansion, bases, near, factor):
    rows, points = near.shape
    strip = left.shape[1]
    rank = bases.shape[0]
    width = OUT_BLOCKS * SUB
    whole = lambda a: pl.BlockSpec(a.shape, lambda step: (0, 0), pipeline_mode=pl.Buffered(1))

    def kernel(*refs):
        out = refs[6]
        flat = out.reshape(rows * PAD, LANES)
        rest_kernel(factor, *refs[:6], flat, *refs[7:])

    return pl.pallas_call(
        kernel,
        grid=(points // width,),
        in_specs=[whole(a) for a in (left, right, target, expansion, bases)]
        + [pl.BlockSpec((rows, width), lambda step: (0, step))],
        out_specs=pl.BlockSpec((rows, 1, PAD, LANES), lambda step: (0, step, 0, 0)),
        out_shape=jax.ShapeDtypeStruct((rows, points // width, PAD, LANES), F32),
        scratch_shapes=[
            pltpu.VMEM((rows, 2 * strip), BF),
            pltpu.VMEM((rows, 2 * strip), F8),
            pltpu.VMEM((rows, 2 * strip), F8),
            pltpu.VMEM((rows, LANES), F32),
            pltpu.VMEM((rows, 3 * rank), BF),
            pltpu.VMEM((3 * rank, points), BF),
            pltpu.VMEM((FEATS, 2 * strip), F32),
            pltpu.VMEM((2 * strip, FEATS), BF),
        ]
        + weight_scratch(2 * strip),
        compiler_params=pltpu.CompilerParams(vmem_limit_bytes=LIMIT),
        cost_estimate=pl.CostEstimate(
            flops=10_000_000_000, bytes_accessed=21_000_000, transcendentals=2_000_000
        ),
        name="finish",
    )(left, right, target, expansion, bases, near)


def body(charges, ordering, jitter, leaf_bases, transfer, coupling):
    set_count, vector_count = (charges.shape[0], charges.shape[1])
    points = charges.shape[4]
    row_count = set_count * vector_count
    near_scale = points ** (-0.5)
    leaf_basis = leaf_bases.reshape(leaf_bases.shape[2], points)
    high, high8, low8, unit, tail, head, moment, own_source, target_rows = prepare(
        charges.reshape(row_count * (points // LANES), LANES),
        ordering.reshape(1, points),
        jitter.reshape(3, 1, points),
        leaf_basis,
    )
    count = lax.axis_size("leaf")
    onward = [(i, i + 1) for i in range(count - 1)]
    back = [(i + 1, i) for i in range(count - 1)]
    left = lax.ppermute(tail, "leaf", onward)
    right = lax.ppermute(head, "leaf", back)
    near_part = own_near(high, high8, low8, unit, own_source, target_rows)
    leaf_levels = lax.axis_size("leaf").bit_length() - 1
    sub_levels = lax.axis_size("sub").bit_length() - 1
    position = lax.axis_index("leaf")
    siblings = []
    branch_bits = []
    current = moment
    for bit_index in range(leaf_levels):
        sibling = swapped(current, "leaf", bit_index)
        branch_bit = position >> bit_index & 1
        current = lift_pair(current, sibling, branch_bit, transfer[bit_index])
        siblings.append(sibling)
        branch_bits.append(branch_bit)
    sub_position = lax.axis_index("sub")
    for bit_index in range(sub_levels):
        level_index = leaf_levels + bit_index
        sibling = swapped(current, "sub", bit_index)
        branch_bit = sub_position >> bit_index & 1
        current = lift_pair(current, sibling, branch_bit, transfer[level_index])
        siblings.append(sibling)
        branch_bits.append(branch_bit)
    expansion = jnp.zeros((row_count, moment.shape[1]), jnp.float32)
    for level_index in reversed(range(leaf_levels + sub_levels)):
        couple_mat = lax.dynamic_index_in_dim(
            coupling[level_index], branch_bits[level_index], 0, keepdims=False
        )
        transfer_mat = lax.dynamic_index_in_dim(
            transfer[level_index], branch_bits[level_index], 0, keepdims=False
        )
        expansion = contract_last(siblings[level_index], couple_mat) + contract_last(
            expansion, transfer_mat
        )
    potential = finish(
        left, right, target_rows, expansion, leaf_basis, near_part, near_scale / GAIN
    )
    return potential.reshape(set_count, vector_count, 1, 1, points)


def solution(mesh):
    in_specs = (
        P(None, None, "sub", "leaf", None),
        P("sub", "leaf", None),
        P(None, "sub", "leaf", None),
        P("sub", "leaf", None, None),
        P(),
        P(),
    )
    out_specs = P(None, None, "sub", "leaf", None)
    return jax.shard_map(body, mesh=mesh, in_specs=in_specs, out_specs=out_specs, check_vma=False)
```

```python
import jax
import jax.numpy as jnp
from jax import lax
from jax.experimental import pallas as pl
from jax.experimental.pallas import tpu as pltpu
from jax.sharding import PartitionSpec as P

DELTA_SQ = 0.0025
F8 = jnp.float8_e4m3fn
BF = jnp.bfloat16
F32 = jnp.float32
GAIN = 16.0
TOP = 384.0
FEATS = 32
SUB = 256
OUT_BLOCKS = 4
LANES = 128
PAD = 8
LIMIT = 60 * 1024 * 1024


def mm(left, right):
    return jnp.dot(left, right, preferred_element_type=F32)


def mm_nt(left, right):
    return lax.dot_general(left, right, (((1,), (1,)), ((), ())), preferred_element_type=F32)


def split(value):
    high = value.astype(BF)
    return high, value - high.astype(F32)


def features(coords, source_ref, target_ref, columns):
    ones = jnp.ones_like(coords[0])
    norm = sum(coord * coord for coord in coords)

    def pieces(value):
        out = []
        for _ in range(3):
            high, value = split(value)
            out.append(high.astype(F32))
        return out

    source = []
    target = []
    for coord in coords:
        part = pieces(coord)
        for left, right in ((0, 0), (0, 1), (1, 0), (1, 1), (0, 2), (2, 0)):
            source.append(part[left])
            target.append(-2.0 * part[right])
    source += pieces(norm + DELTA_SQ / (GAIN * GAIN)) + [ones] * 3
    target += [ones] * 3 + pieces(norm)
    blank = [jnp.zeros_like(norm)] * (FEATS - len(source))
    for ref, rows in ((source_ref, source + blank), (target_ref, target + blank)):
        if ref is not None:
            for index, row in enumerate(rows):
                ref[index : index + 1, columns] = row


def scaled(rows):
    top = jnp.maximum(jnp.max(jnp.abs(rows), axis=1, keepdims=True), 1e-30)
    full = rows * (TOP / top)
    high = full.astype(BF)
    return full, high, full - high.astype(F32), top * (1.0 / TOP)


def prepare_kernel(
    q_ref, order_ref, jitter_ref, bases_ref,
    qh_ref, q8h_ref, q8l_ref, unit_ref, tail_ref, head_ref, moment_ref, feat_ref, target_ref,
    pick, pick8, basis, moved, source_rows, target_rows,
):
    points = order_ref.shape[1]
    strip = tail_ref.shape[1]
    rank = bases_ref.shape[0]
    chunk = qh_ref.shape[0]
    tiles = points // LANES
    last = points - strip
    now = pl.program_id(0)

    @pl.when(now == 0)
    def _():
        index = lax.broadcasted_iota(jnp.int32, (1, points), 1).astype(F32)
        coords = [(index + jitter_ref[0]) * (1.0 / points), jitter_ref[1], jitter_ref[2]]
        coords = [(coord - 0.5) * (1.0 / GAIN) for coord in coords]
        features(coords, source_rows, target_rows, slice(0, points))
        target_ref[...] = target_rows[...].astype(BF)
        rows = tail_ref.shape[0] - PAD
        for axis in range(3):
            tail_ref[rows + axis : rows + axis + 1, :] = coords[axis][:, last:]
            head_ref[rows + axis : rows + axis + 1, :] = coords[axis][:, :strip]
        blank = jnp.zeros((PAD - 3, strip), F32)
        tail_ref[rows + 3 :, :] = blank
        head_ref[rows + 3 :, :] = blank
        high, low = split(bases_ref[...])
        moved[:rank, :] = high
        moved[rank : 2 * rank, :] = low.astype(BF)
        moved[2 * rank :, :] = source_rows[...].astype(BF)

        @pl.loop(0, points // SUB)
        def _(step):
            rows = pl.ds(pl.multiple_of(step * SUB, SUB), SUB)
            own = lax.broadcasted_iota(jnp.int32, (SUB, strip), 0) + step * SUB
            for part in range(points // strip):
                columns = slice(part * strip, (part + 1) * strip)
                hit = jnp.where(own == order_ref[:, columns], 1.0, 0.0)
                pick[rows, columns] = hit.astype(BF)
                if part == 0:
                    pick8[rows, :strip] = hit.astype(F8)
                if part == points // strip - 1:
                    pick8[rows, strip:] = hit.astype(F8)
            placed = mm_nt(pick[rows, :], moved[...]).astype(BF)
            feat_ref[rows, :] = placed[:, 2 * rank :]
            basis[rows, :] = placed[:, : 2 * rank]

    block = [q_ref[pl.ds(tile, chunk, stride=tiles), :] for tile in range(tiles)]
    full, high, rest, unit = scaled(jnp.concatenate(block, axis=1))
    low8 = rest.astype(F8)
    qh_ref[...] = high
    q8h_ref[...] = full.astype(F8)
    q8l_ref[...] = low8
    unit_ref[...] = jnp.broadcast_to(unit, unit_ref.shape)
    rows = pl.ds(pl.multiple_of(now * chunk, chunk), chunk)
    head_ref[rows, :] = (mm(high, pick[:, :strip]) + mm(low8, pick8[:, :strip])) * unit
    tail_ref[rows, :] = (mm(high, pick[:, last:]) + mm(low8, pick8[:, strip:])) * unit
    both = mm(high, basis[...])
    moment_ref[...] = (
        both[:, :rank] + both[:, rank:] + mm(rest.astype(BF), basis[:, :rank])
    ) * unit


def prepare(charges, order, jitter, bases):
    points = order.shape[1]
    tiles = points // LANES
    rows = charges.shape[0] // tiles
    strip = points // 4
    rank = bases.shape[0]
    chunk = 256
    whole = lambda shape: pl.BlockSpec(shape, lambda step: (0,) * len(shape))
    sliced = lambda width: pl.BlockSpec((chunk, width), lambda step: (step, 0))
    shape = jax.ShapeDtypeStruct
    return pl.pallas_call(
        prepare_kernel,
        grid=(rows // chunk,),
        in_specs=[
            pl.BlockSpec((chunk * tiles, LANES), lambda step: (step, 0)),
            whole(order.shape),
            whole(jitter.shape),
            whole(bases.shape),
        ],
        out_specs=[sliced(points)] * 3
        + [sliced(LANES), whole((rows + PAD, strip)), whole((rows + PAD, strip)), sliced(rank)]
        + [whole((points, FEATS)), whole((FEATS, points))],
        out_shape=[
            shape((rows, points), BF),
            shape((rows, points), F8),
            shape((rows, points), F8),
            shape((rows, LANES), F32),
            shape((rows + PAD, strip), F32),
            shape((rows + PAD, strip), F32),
            shape((rows, rank), F32),
            shape((points, FEATS), BF),
            shape((FEATS, points), BF),
        ],
        scratch_shapes=[
            pltpu.VMEM((points, points), BF),
            pltpu.VMEM((points, 2 * strip), F8),
            pltpu.VMEM((points, 2 * rank), BF),
            pltpu.VMEM((2 * rank + FEATS, points), BF),
            pltpu.VMEM((FEATS, points), F32),
            pltpu.VMEM((FEATS, points), F32),
        ],
        compiler_params=pltpu.CompilerParams(vmem_limit_bytes=LIMIT),
        cost_estimate=pl.CostEstimate(
            flops=14_000_000_000, bytes_accessed=28_000_000, transcendentals=0
        ),
        name="prepare",
    )(charges, order, jitter, bases)


def weigh(source_ref, target, first, last, slot, w, w8h, w8l):
    for row in range(first, last, 128):
        rows = slice(row, row + 128)
        weight = lax.rsqrt(mm(source_ref[rows, :], target))
        high = weight.astype(BF)
        w[slot, rows, :] = high
        w8h[slot, rows, :] = weight.astype(F8)
        w8l[slot, rows, :] = (weight - high.astype(F32)).astype(F8)


def sweep(source_ref, target_ref, row_count, w, w8h, w8l, emit, count, between=None):
    points = source_ref.shape[0]
    blocks = target_ref.shape[1] // SUB
    step = pl.program_id(0)
    parts = 4

    def target(block):
        return target_ref[:, pl.ds(pl.multiple_of(block * SUB, SUB), SUB)]

    @pl.when(step == 0)
    def _():
        weigh(source_ref, target(0), 0, points, 0, w, w8h, w8l)

    height = row_count // parts
    for block in range(count):
        slot = block % 2
        coming = target(jnp.minimum(count * step + block + 1, blocks - 1))
        for part in range(parts):
            weigh(
                source_ref,
                coming,
                part * points // parts,
                (part + 1) * points // parts,
                1 - slot,
                w,
                w8h,
                w8l,
            )
            emit(slice(part * height, (part + 1) * height), block, slot)
        if between is not None:
            between(step, block)


def fine(left, right, product):
    left_high, left_low = split(left)
    right_high, right_low = split(right)
    low = product(left_low.astype(BF), right_high) + product(left_high, right_low.astype(BF))
    return product(left_high, right_high) + low


class Stage:
    def __init__(self, axis, shift, bits, level, rows):
        self.axis = axis
        self.shift = shift
        self.bits = bits
        self.level = level
        self.size = 1 << bits
        self.rows = rows
        self.share = rows // self.size

    def scratch(self, rank):
        return [
            pltpu.VMEM((self.size, self.share, rank), F32),
            pltpu.VMEM((self.size, self.share, rank), F32),
            pltpu.VMEM((self.size, self.share, rank), F32),
            pltpu.VMEM((self.size, self.share, rank), F32),
            pltpu.VMEM((self.share, rank), F32),
        ] + [pltpu.SemaphoreType.DMA((self.size - 1,))] * 4

    def place(self):
        position = lax.axis_index(self.axis)
        member = lax.rem(position // (1 << self.shift), self.size)
        return position, member

    def partner(self, offset):
        position, member = self.place()
        peer = lax.rem(member + offset, self.size)
        return peer, {self.axis: position + (peer - member) * (1 << self.shift)}

    def bind(self, refs):
        self.gathered, self.middle, self.outgoing, self.returned, self.top = refs[:5]
        self.semaphores = refs[5:]

    def upward(self, source):
        _, member = self.place()
        out = []
        for offset in range(1, self.size):
            peer, device = self.partner(offset)
            rows = pl.ds(pl.multiple_of(peer * self.share, self.share), self.share)
            out.append(
                pltpu.make_async_remote_copy(
                    src_ref=source.at[rows, :],
                    dst_ref=self.gathered.at[member],
                    send_sem=self.semaphores[0].at[offset - 1],
                    recv_sem=self.semaphores[1].at[offset - 1],
                    device_id=device,
                    device_id_type=pl.DeviceIdType.MESH,
                )
            )
        return out

    def downward(self):
        _, member = self.place()
        out = []
        for offset in range(1, self.size):
            peer, device = self.partner(offset)
            out.append(
                pltpu.make_async_remote_copy(
                    src_ref=self.outgoing.at[peer],
                    dst_ref=self.returned.at[member],
                    send_sem=self.semaphores[2].at[offset - 1],
                    recv_sem=self.semaphores[3].at[offset - 1],
                    device_id=device,
                    device_id_type=pl.DeviceIdType.MESH,
                )
            )
        return out

    def send_up(self, source):
        for copy in self.upward(source):
            copy.start()
        _, member = self.place()
        rows = pl.ds(pl.multiple_of(member * self.share, self.share), self.share)
        self.gathered[member] = source[rows, :]

    def send_down(self):
        for copy in self.downward():
            copy.start()
        _, member = self.place()
        self.returned[member] = self.outgoing[member]

    def levels(self, source, transfer_ref, last):
        for copy in self.upward(source):
            copy.wait_recv()
        nodes = [self.gathered[index] for index in range(self.size)]
        first = 0
        for step in range(self.bits):
            if last and step == self.bits - 1:
                break
            level = self.level + step
            even = jnp.concatenate(nodes[0::2], axis=0)
            odd = jnp.concatenate(nodes[1::2], axis=0)
            parents = fine(even, transfer_ref[level, 0], mm) + fine(odd, transfer_ref[level, 1], mm)
            nodes = [
                parents[index * self.share : (index + 1) * self.share]
                for index in range(len(nodes) // 2)
            ]
            if step < self.bits - 1:
                for index, value in enumerate(nodes):
                    self.middle[first + index] = value
                first += len(nodes)
            else:
                self.top[...] = nodes[0]

    def expand(self, parent, transfer_ref, coupling_ref):
        expansions = [parent]
        starts = []
        first = 0
        for step in range(1, self.bits):
            starts.append(first)
            first += self.size >> step
        for step in reversed(range(self.bits)):
            level = self.level + step
            held = self.gathered if step == 0 else self.middle
            base = 0 if step == 0 else starts[step - 1]
            count = self.size >> step
            results = [None] * count
            for side in range(2):
                sibling = jnp.concatenate(
                    [held[base + index] for index in range(1 - side, count, 2)], axis=0
                )
                value = fine(sibling, coupling_ref[level, side], mm_nt)
                if expansions[0] is not None:
                    above = jnp.concatenate(expansions, axis=0)
                    value = value + fine(above, transfer_ref[level, side], mm_nt)
                for index in range(count // 2):
                    results[2 * index + side] = value[
                        index * self.share : (index + 1) * self.share
                    ]
            expansions = results
        for index, value in enumerate(expansions):
            self.outgoing[index] = value

    def arrived(self):
        for copy in self.downward():
            copy.wait_recv()
        return jnp.concatenate([self.returned[index] for index in range(self.size)], axis=0)

    def sent(self, source):
        for copy in self.upward(source) + self.downward():
            copy.wait_send()


def own_kernel(
    stages, qh_ref, q8h_ref, q8l_ref, unit_ref, source_ref, target_ref, moment_ref, transfer_ref,
    coupling_ref, tail_ref, head_ref, out_ref, expansion_ref, left_ref, right_ref,
    w, w8h, w8l, edge_sems, *stage_refs,
):
    per_stage = len(stage_refs) // len(stages)
    for index, stage in enumerate(stages):
        stage.bind(stage_refs[index * per_stage : (index + 1) * per_stage])
    low, middle, high = stages
    position = lax.axis_index("leaf")
    count = lax.axis_size("leaf")
    after = {"leaf": lax.rem(position + 1, count)}
    before = {"leaf": lax.rem(position + count - 1, count)}

    def edges():
        return [
            pltpu.make_async_remote_copy(
                src_ref=source,
                dst_ref=target,
                send_sem=edge_sems.at[index],
                recv_sem=edge_sems.at[2 + index],
                device_id=device,
                device_id_type=pl.DeviceIdType.MESH,
            )
            for index, (source, target, device) in enumerate(
                ((tail_ref, left_ref, after), (head_ref, right_ref, before))
            )
        ]

    @pl.when(pl.program_id(0) == 0)
    def _():
        barrier = pltpu.get_barrier_semaphore()
        devices = [before, after]
        for stage in stages:
            devices += [stage.partner(offset)[1] for offset in range(1, stage.size)]
        for device in devices:
            pl.semaphore_signal(
                barrier, inc=1, device_id=device, device_id_type=pl.DeviceIdType.MESH
            )
        pl.semaphore_wait(barrier, len(devices))
        low.send_up(moment_ref)
        for copy in edges():
            copy.start()

    def emit(rows, block, slot):
        total = mm(qh_ref[rows, :], w[slot])
        total = total + mm(q8h_ref[rows, :], w8l[slot])
        total = total + mm(q8l_ref[rows, :], w8h[slot])
        out_ref[rows, block * SUB : (block + 1) * SUB] = total * unit_ref[rows, 0:1]

    def between(step, block):
        def at(number):
            return pl.when(step == number)

        if block == 1:

            @at(0)
            def _():
                low.levels(moment_ref, transfer_ref, False)
                middle.send_up(low.top)

            @at(1)
            def _():
                high.levels(middle.top, transfer_ref, True)
                high.expand(None, transfer_ref, coupling_ref)
                high.send_down()

            @at(2)
            def _():
                low.expand(middle.arrived(), transfer_ref, coupling_ref)
                low.send_down()

            @at(3)
            def _():
                expansion_ref[...] = low.arrived()
                low.sent(moment_ref)
                middle.sent(low.top)
                high.sent(middle.top)
                for copy in edges():
                    copy.wait()

        else:

            @at(1)
            def _():
                middle.levels(low.top, transfer_ref, False)
                high.send_up(middle.top)

            @at(2)
            def _():
                middle.expand(high.arrived(), transfer_ref, coupling_ref)
                middle.send_down()

    sweep(source_ref, target_ref, out_ref.shape[0], w, w8h, w8l, emit, 2, between)


def weight_scratch(count):
    return [
        pltpu.VMEM((2, count, SUB), BF),
        pltpu.VMEM((2, count, SUB), F8),
        pltpu.VMEM((2, count, SUB), F8),
    ]


def own_near(high, high8, low8, unit, source, target, moment, transfer, coupling, tail, head):
    rows, points = high.shape
    rank = moment.shape[1]
    leaf_bits = lax.axis_size("leaf").bit_length() - 1
    sub_bits = lax.axis_size("sub").bit_length() - 1
    near_bits = leaf_bits - leaf_bits // 2
    stages = []
    height = rows
    level = 0
    for axis, shift, bits in (
        ("leaf", 0, near_bits),
        ("leaf", near_bits, leaf_bits - near_bits),
        ("sub", 0, sub_bits),
    ):
        stages.append(Stage(axis, shift, bits, level, height))
        level += bits
        height = stages[-1].share
    whole = lambda a: pl.BlockSpec(
        a.shape, lambda step: (0,) * len(a.shape), pipeline_mode=pl.Buffered(1)
    )
    far = pl.BlockSpec(memory_space=pl.ANY)
    near = (high, high8, low8, unit, source, target, moment, transfer, coupling)
    scratch = []
    for stage in stages:
        scratch += stage.scratch(rank)
    return pl.pallas_call(
        lambda *refs: own_kernel(stages, *refs),
        grid=(points // (2 * SUB),),
        in_specs=[whole(a) for a in near] + [far, far],
        out_specs=[
            pl.BlockSpec((rows, 2 * SUB), lambda step: (0, step)),
            pl.BlockSpec((rows, rank), lambda step: (0, 0)),
            far,
            far,
        ],
        out_shape=[
            jax.ShapeDtypeStruct((rows, points), F32),
            jax.ShapeDtypeStruct((rows, rank), F32),
            jax.ShapeDtypeStruct(tail.shape, F32),
            jax.ShapeDtypeStruct(head.shape, F32),
        ],
        scratch_shapes=weight_scratch(points) + [pltpu.SemaphoreType.DMA((4,))] + scratch,
        compiler_params=pltpu.CompilerParams(
            vmem_limit_bytes=LIMIT, collective_id=0, has_side_effects=True
        ),
        cost_estimate=pl.CostEstimate(
            flops=17_000_000_000, bytes_accessed=24_000_000, transcendentals=4_000_000
        ),
        name="own_near",
    )(*near, tail, head)


def rest_kernel(
    factor, left_ref, right_ref, edge_ref, target_ref, expansion_ref, bases_ref, near_ref,
    out_ref, qh, q8h, q8l, units, far, basis, source_rows, source, w, w8h, w8l,
):
    strip = left_ref.shape[1]
    rank = expansion_ref.shape[1]
    row_count = near_ref.shape[0]

    @pl.when(pl.program_id(0) == 0)
    def _():
        for ref, shift, columns in (
            (left_ref, -1.0, slice(0, strip)),
            (right_ref, 1.0, slice(strip, 2 * strip)),
        ):
            coords = [ref[row_count + axis : row_count + axis + 1, :] for axis in range(3)]
            coords[0] = coords[0] + shift / GAIN
            features(coords, source_rows, None, columns)
        source[...] = jnp.transpose(source_rows[...]).astype(BF)

        @pl.loop(0, row_count // SUB)
        def _(step):
            rows = pl.ds(pl.multiple_of(step * SUB, SUB), SUB)
            joined = jnp.concatenate(
                [left_ref[rows, :] * edge_ref[0:1, 0:1], right_ref[rows, :] * edge_ref[1:2, 0:1]],
                axis=1,
            )
            full, high, rest, unit = scaled(joined)
            qh[rows, :] = high
            q8h[rows, :] = full.astype(F8)
            q8l[rows, :] = rest.astype(F8)
            units[rows, :] = jnp.broadcast_to(unit, (SUB, units.shape[1]))
            top, low = split(expansion_ref[rows, :])
            far[rows, :rank] = top
            far[rows, rank : 2 * rank] = low.astype(BF)
            far[rows, 2 * rank :] = top

        top, low = split(bases_ref[...])
        basis[:rank, :] = top
        basis[rank : 2 * rank, :] = top
        basis[2 * rank :, :] = low.astype(BF)

    def emit(rows, block, slot):
        total = mm(qh[rows, :], w[slot])
        total = total + mm(q8h[rows, :], w8l[slot])
        total = total + mm(q8l[rows, :], w8h[slot])
        inner = slice(block * SUB, (block + 1) * SUB)
        total = total * units[rows, 0:1] + near_ref[rows, inner]
        columns = pl.ds(
            pl.multiple_of((pl.program_id(0) * OUT_BLOCKS + block) * SUB, SUB), SUB
        )
        total = total * factor + mm(far[rows, :], basis[:, columns])
        first = rows.start * PAD
        for part in range(SUB // LANES):
            place = first + block * (SUB // LANES) + part
            out_ref[pl.ds(place, rows.stop - rows.start, stride=PAD), :] = total[
                :, part * LANES : (part + 1) * LANES
            ]

    sweep(source, target_ref, row_count, w, w8h, w8l, emit, OUT_BLOCKS)


def finish(left, right, edge, target, expansion, bases, near, factor):
    rows, points = near.shape
    strip = left.shape[1]
    rank = bases.shape[0]
    width = OUT_BLOCKS * SUB
    whole = lambda a: pl.BlockSpec(a.shape, lambda step: (0, 0), pipeline_mode=pl.Buffered(1))

    def kernel(*refs):
        out = refs[7]
        flat = out.reshape(rows * PAD, LANES)
        rest_kernel(factor, *refs[:7], flat, *refs[8:])

    return pl.pallas_call(
        kernel,
        grid=(points // width,),
        in_specs=[whole(a) for a in (left, right, edge, target, expansion, bases)]
        + [pl.BlockSpec((rows, width), lambda step: (0, step))],
        out_specs=pl.BlockSpec((rows, 1, PAD, LANES), lambda step: (0, step, 0, 0)),
        out_shape=jax.ShapeDtypeStruct((rows, points // width, PAD, LANES), F32),
        scratch_shapes=[
            pltpu.VMEM((rows, 2 * strip), BF),
            pltpu.VMEM((rows, 2 * strip), F8),
            pltpu.VMEM((rows, 2 * strip), F8),
            pltpu.VMEM((rows, LANES), F32),
            pltpu.VMEM((rows, 3 * rank), BF),
            pltpu.VMEM((3 * rank, points), BF),
            pltpu.VMEM((FEATS, 2 * strip), F32),
            pltpu.VMEM((2 * strip, FEATS), BF),
        ]
        + weight_scratch(2 * strip),
        compiler_params=pltpu.CompilerParams(vmem_limit_bytes=LIMIT),
        cost_estimate=pl.CostEstimate(
            flops=10_000_000_000, bytes_accessed=21_000_000, transcendentals=2_000_000
        ),
        name="finish",
    )(left, right, edge, target, expansion, bases, near)


def body(charges, ordering, jitter, leaf_bases, transfer, coupling):
    set_count, vector_count = (charges.shape[0], charges.shape[1])
    points = charges.shape[4]
    row_count = set_count * vector_count
    near_scale = points ** (-0.5)
    leaf_basis = leaf_bases.reshape(leaf_bases.shape[2], points)
    high, high8, low8, unit, tail, head, moment, own_source, target_rows = prepare(
        charges.reshape(row_count * (points // LANES), LANES),
        ordering.reshape(1, points),
        jitter.reshape(3, 1, points),
        leaf_basis,
    )
    near_part, expansion, left, right = own_near(
        high, high8, low8, unit, own_source, target_rows, moment, transfer, coupling, tail, head
    )
    position = lax.axis_index("leaf")
    inner = jnp.stack([position > 0, position < lax.axis_size("leaf") - 1])
    edge = jnp.broadcast_to(inner[:, None].astype(F32), (2, LANES))
    potential = finish(
        left, right, edge, target_rows, expansion, leaf_basis, near_part, near_scale / GAIN
    )
    return potential.reshape(set_count, vector_count, 1, 1, points)


def solution(mesh):
    in_specs = (
        P(None, None, "sub", "leaf", None),
        P("sub", "leaf", None),
        P(None, "sub", "leaf", None),
        P("sub", "leaf", None, None),
        P(),
        P(),
    )
    out_specs = P(None, None, "sub", "leaf", None)
    return jax.shard_map(body, mesh=mesh, in_specs=in_specs, out_specs=out_specs, check_vma=False)
```

```python
import jax
import jax.numpy as jnp
from jax import lax
from jax.experimental import pallas as pl
from jax.experimental.pallas import tpu as pltpu
from jax.sharding import PartitionSpec as P

DELTA_SQ = 0.0025
F8 = jnp.float8_e4m3fn
BF = jnp.bfloat16
F32 = jnp.float32
GAIN = 16.0
TOP = 384.0
FEATS = 32
SUB = 256
OUT_BLOCKS = 4
LANES = 128
PAD = 8
LIMIT = 60 * 1024 * 1024


def mm(left, right):
    return jnp.dot(left, right, preferred_element_type=F32)


def mm_nt(left, right):
    return lax.dot_general(left, right, (((1,), (1,)), ((), ())), preferred_element_type=F32)


def split(value):
    high = value.astype(BF)
    return high, value - high.astype(F32)


def features(coords, source_ref, target_ref, columns):
    ones = jnp.ones_like(coords[0])
    norm = sum(coord * coord for coord in coords)

    def pieces(value):
        out = []
        for _ in range(3):
            high, value = split(value)
            out.append(high.astype(F32))
        return out

    source = []
    target = []
    for coord in coords:
        part = pieces(coord)
        for left, right in ((0, 0), (0, 1), (1, 0), (1, 1), (0, 2), (2, 0)):
            source.append(part[left])
            target.append(-2.0 * part[right])
    source += pieces(norm + DELTA_SQ / (GAIN * GAIN)) + [ones] * 3
    target += [ones] * 3 + pieces(norm)
    blank = [jnp.zeros_like(norm)] * (FEATS - len(source))
    for ref, rows in ((source_ref, source + blank), (target_ref, target + blank)):
        if ref is not None:
            for index, row in enumerate(rows):
                ref[index : index + 1, columns] = row


def scaled(rows):
    top = jnp.maximum(jnp.max(jnp.abs(rows), axis=1, keepdims=True), 1e-30)
    full = rows * (TOP / top)
    high = full.astype(BF)
    return full, high, full - high.astype(F32), top * (1.0 / TOP)


def weigh(source_ref, target, first, last, slot, w, w8h, w8l):
    for row in range(first, last, 128):
        rows = slice(row, row + 128)
        weight = lax.rsqrt(mm(source_ref[rows, :], target))
        high = weight.astype(BF)
        w[slot, rows, :] = high
        w8h[slot, rows, :] = weight.astype(F8)
        w8l[slot, rows, :] = (weight - high.astype(F32)).astype(F8)


def sweep(source_ref, target_ref, row_count, w, w8h, w8l, emit, count, step):
    points = source_ref.shape[0]
    blocks = target_ref.shape[1] // SUB
    parts = 4

    def target(block):
        return target_ref[:, pl.ds(pl.multiple_of(block * SUB, SUB), SUB)]

    @pl.when(step == 0)
    def _():
        weigh(source_ref, target(0), 0, points, 0, w, w8h, w8l)

    height = row_count // parts
    for block in range(count):
        slot = block % 2
        coming = target(jnp.minimum(count * step + block + 1, blocks - 1))
        for part in range(parts):
            weigh(
                source_ref,
                coming,
                part * points // parts,
                (part + 1) * points // parts,
                1 - slot,
                w,
                w8h,
                w8l,
            )
            emit(slice(part * height, (part + 1) * height), block, slot)


def fine(left, right, product):
    left_high, left_low = split(left)
    right_high, right_low = split(right)
    low = product(left_low.astype(BF), right_high) + product(left_high, right_low.astype(BF))
    return product(left_high, right_high) + low


def pack(value):
    half = value.shape[0] // 2
    return jnp.concatenate([value[:half], value[half:]], axis=1)


def unpack(value):
    half = value.shape[1] // 2
    return jnp.concatenate([value[:, :half], value[:, half:]], axis=0)


class Stage:
    def __init__(self, axis, shift, bits, level):
        self.axis = axis
        self.shift = shift
        self.bits = bits
        self.level = level
        self.size = 1 << bits

    def scratch(self, share, rank):
        width = (share // 2, 2 * rank)
        count = self.size - 1
        return [
            pltpu.VMEM((self.size,) + width, F32),
            pltpu.VMEM((max(self.size - 2, 1), share, rank), F32),
            pltpu.VMEM((self.size,) + width, F32),
            pltpu.VMEM((self.size,) + width, F32),
            pltpu.VMEM(width, F32),
        ] + [pltpu.SemaphoreType.DMA((count,))] * 4

    def bind(self, refs):
        self.gathered, self.middle, self.outgoing, self.returned, self.top = refs[:5]
        self.semaphores = refs[5:]

    def member(self):
        return lax.rem(lax.axis_index(self.axis) // (1 << self.shift), self.size)

    def partner(self, offset):
        position = lax.axis_index(self.axis)
        peer = lax.rem(self.member() + offset, self.size)
        return peer, {self.axis: position + (peer - self.member()) * (1 << self.shift)}

    def copies(self, source, target, sems):
        out = []
        for offset in range(1, self.size):
            peer, device = self.partner(offset)
            out.append(
                pltpu.make_async_remote_copy(
                    src_ref=source.at[peer] if len(source.shape) == 3 else source,
                    dst_ref=target.at[self.member()],
                    send_sem=self.semaphores[sems].at[offset - 1],
                    recv_sem=self.semaphores[sems + 1].at[offset - 1],
                    device_id=device,
                    device_id_type=pl.DeviceIdType.MESH,
                )
            )
        return out

    def upward(self, source):
        return self.copies(source, self.gathered, 0)

    def downward(self):
        return self.copies(self.outgoing, self.returned, 2)

    def send_up(self, source):
        for copy in self.upward(source):
            copy.start()
        member = self.member()
        self.gathered[member] = source[member] if len(source.shape) == 3 else source[...]

    def send_down(self):
        for copy in self.downward():
            copy.start()
        member = self.member()
        self.returned[member] = self.outgoing[member]

    def levels(self, source, transfer_ref, last):
        for copy in self.upward(source):
            copy.wait_recv()
        share = self.middle.shape[1]
        nodes = [unpack(self.gathered[index]) for index in range(self.size)]
        first = 0
        for step in range(self.bits - 1 if last else self.bits):
            level = self.level + step
            even = jnp.concatenate(nodes[0::2], axis=0)
            odd = jnp.concatenate(nodes[1::2], axis=0)
            parents = fine(even, transfer_ref[level, 0], mm) + fine(odd, transfer_ref[level, 1], mm)
            nodes = [
                parents[index * share : (index + 1) * share] for index in range(len(nodes) // 2)
            ]
            if step < self.bits - 1:
                for index, value in enumerate(nodes):
                    self.middle[first + index] = value
                first += len(nodes)
            else:
                self.top[...] = pack(nodes[0])

    def expand(self, parent, transfer_ref, coupling_ref):
        share = self.middle.shape[1]
        expansions = [parent]
        starts = [0]
        for step in range(1, self.bits):
            starts.append(starts[-1] + (self.size >> step))
        for step in reversed(range(self.bits)):
            level = self.level + step
            count = self.size >> step
            if step == 0:
                held = [unpack(self.gathered[index]) for index in range(count)]
            else:
                held = [self.middle[starts[step - 1] + index] for index in range(count)]
            results = [None] * count
            for side in range(2):
                sibling = jnp.concatenate(held[1 - side :: 2], axis=0)
                value = fine(sibling, coupling_ref[level, side], mm_nt)
                if expansions[0] is not None:
                    above = jnp.concatenate(expansions, axis=0)
                    value = value + fine(above, transfer_ref[level, side], mm_nt)
                for index in range(count // 2):
                    results[2 * index + side] = value[index * share : (index + 1) * share]
            expansions = results
        for index, value in enumerate(expansions):
            self.outgoing[index] = pack(value)

    def chosen(self):
        return unpack(self.outgoing[self.member()])

    def arrived(self):
        for copy in self.downward():
            copy.wait_recv()
        return jnp.concatenate([unpack(self.returned[i]) for i in range(self.size)], axis=0)


def own_kernel(
    stages, q_ref, order_ref, jitter_ref, bases_ref, transfer_ref, coupling_ref,
    out_ref, target_out, expansion_ref, left_ref, right_ref,
    pick, pick8, basis, moved, source_rows, target_rows, feat, target, qh, q8h, q8l, unit_ref,
    tail, head, packed, edge_sems, w, w8h, w8l, *stage_refs,
):
    per_stage = len(stage_refs) // len(stages)
    for index, stage in enumerate(stages):
        stage.bind(stage_refs[index * per_stage : (index + 1) * per_stage])
    low, middle, high = stages
    points = order_ref.shape[1]
    strip = tail.shape[1]
    rank = bases_ref.shape[0]
    row_count = qh.shape[0]
    tiles = points // LANES
    chunk = q_ref.shape[0] // tiles
    chunks = row_count // chunk
    last = points - strip
    now = pl.program_id(0)
    position = lax.axis_index("leaf")
    count = lax.axis_size("leaf")
    after = {"leaf": lax.rem(position + 1, count)}
    before = {"leaf": lax.rem(position + count - 1, count)}

    def edges(first, height, slot):
        rows = pl.ds(first, height)
        return [
            pltpu.make_async_remote_copy(
                src_ref=source.at[rows, :],
                dst_ref=target.at[rows, :],
                send_sem=edge_sems.at[2 * index, slot],
                recv_sem=edge_sems.at[2 * index + 1, slot],
                device_id=device,
                device_id_type=pl.DeviceIdType.MESH,
            )
            for index, (source, target, device) in enumerate(
                ((tail, left_ref, after), (head, right_ref, before))
            )
        ]

    @pl.when(now == 0)
    def _():
        barrier = pltpu.get_barrier_semaphore()
        devices = [before, after]
        for stage in stages:
            devices += [stage.partner(offset)[1] for offset in range(1, stage.size)]
        for device in devices:
            pl.semaphore_signal(
                barrier, inc=1, device_id=device, device_id_type=pl.DeviceIdType.MESH
            )

        index = lax.broadcasted_iota(jnp.int32, (1, points), 1).astype(F32)
        coords = [(index + jitter_ref[0]) * (1.0 / points), jitter_ref[1], jitter_ref[2]]
        coords = [(coord - 0.5) * (1.0 / GAIN) for coord in coords]
        features(coords, source_rows, target_rows, slice(0, points))
        target[...] = target_rows[...].astype(BF)
        target_out[...] = target_rows[...].astype(BF)
        for axis in range(3):
            tail[row_count + axis : row_count + axis + 1, :] = coords[axis][:, last:]
            head[row_count + axis : row_count + axis + 1, :] = coords[axis][:, :strip]
        blank = jnp.zeros((PAD - 3, strip), F32)
        tail[row_count + 3 :, :] = blank
        head[row_count + 3 :, :] = blank
        top, rest = split(bases_ref[...])
        moved[:rank, :] = top
        moved[rank : 2 * rank, :] = rest.astype(BF)
        moved[2 * rank :, :] = source_rows[...].astype(BF)

        @pl.loop(0, points // SUB)
        def _(step):
            rows = pl.ds(pl.multiple_of(step * SUB, SUB), SUB)
            own = lax.broadcasted_iota(jnp.int32, (SUB, strip), 0) + step * SUB
            for part in range(points // strip):
                columns = slice(part * strip, (part + 1) * strip)
                hit = jnp.where(own == order_ref[:, columns], 1.0, 0.0)
                pick[rows, columns] = hit.astype(BF)
                if part == 0:
                    pick8[rows, :strip] = hit.astype(F8)
                if part == points // strip - 1:
                    pick8[rows, strip:] = hit.astype(F8)
            placed = mm_nt(pick[rows, :], moved[...]).astype(BF)
            feat[rows, :] = placed[:, 2 * rank :]
            basis[rows, :] = placed[:, : 2 * rank]

        pl.semaphore_wait(barrier, len(devices))

    @pl.when(now < chunks)
    def _():
        rows = pl.ds(pl.multiple_of(now * chunk, chunk), chunk)
        block = [q_ref[pl.ds(tile, chunk, stride=tiles), :] for tile in range(tiles)]
        full, top, rest, unit = scaled(jnp.concatenate(block, axis=1))
        qh[rows, :] = top
        q8h[rows, :] = full.astype(F8)
        q8l[rows, :] = rest.astype(F8)
        unit_ref[rows, :] = jnp.broadcast_to(unit, (chunk, LANES))
        both = mm(top, basis[...])
        moment = (both[:, :rank] + both[:, rank:] + mm(rest.astype(BF), basis[:, :rank])) * unit
        share = row_count // low.size
        for part in range(chunk // share):
            packed[now * (chunk // share) + part] = pack(moment[part * share : (part + 1) * share])

    @pl.when(now == chunks)
    def _():
        low.send_up(packed)
        for copy in edges(row_count, PAD, chunks):
            copy.start()

    @pl.when(jnp.logical_and(now >= chunks, now < 2 * chunks))
    def _():
        part = now - chunks
        first = pl.multiple_of(part * chunk, chunk)
        rows = pl.ds(first, chunk)
        unit = unit_ref[rows, 0:1]
        for target, picked, picked8 in (
            (tail, slice(last, points), slice(strip, 2 * strip)),
            (head, slice(0, strip), slice(0, strip)),
        ):
            target[rows, :] = (
                mm(qh[rows, :], pick[:, picked]) + mm(q8l[rows, :], pick8[:, picked8])
            ) * unit
        for copy in edges(first, chunk, part):
            copy.start()

    @pl.when(now == 2 * chunks - 1)
    def _():
        low.levels(packed, transfer_ref, False)
        middle.send_up(low.top)

    def emit(rows, block, slot):
        total = mm(qh[rows, :], w[slot])
        total = total + mm(q8h[rows, :], w8l[slot])
        total = total + mm(q8l[rows, :], w8h[slot])
        out_ref[rows, block * SUB : (block + 1) * SUB] = total * unit_ref[rows, 0:1]

    @pl.when(now >= 2 * chunks)
    def _():
        sweep(feat, target, row_count, w, w8h, w8l, emit, 2, now - 2 * chunks)

    @pl.when(now == 2 * chunks)
    def _():
        middle.levels(low.top, transfer_ref, False)
        high.send_up(middle.top)

    @pl.when(now == 2 * chunks + 1)
    def _():
        high.levels(middle.top, transfer_ref, True)
        high.expand(None, transfer_ref, coupling_ref)
        middle.expand(high.chosen(), transfer_ref, coupling_ref)
        low.expand(middle.chosen(), transfer_ref, coupling_ref)
        low.send_down()

    @pl.when(now == pl.num_programs(0) - 1)
    def _():
        expansion_ref[...] = low.arrived()
        for copy in low.upward(packed) + low.downward():
            copy.wait_send()
        for copy in middle.upward(low.top) + high.upward(middle.top):
            copy.wait_send()
        for part in range(chunks):
            for copy in edges(part * chunk, chunk, part):
                copy.wait()
        for copy in edges(row_count, PAD, chunks):
            copy.wait()


def weight_scratch(count):
    return [
        pltpu.VMEM((2, count, SUB), BF),
        pltpu.VMEM((2, count, SUB), F8),
        pltpu.VMEM((2, count, SUB), F8),
    ]


def own_near(charges, order, jitter, bases, transfer, coupling):
    points = order.shape[1]
    tiles = points // LANES
    rows = charges.shape[0] // tiles
    strip = points // 4
    rank = bases.shape[0]
    chunk = 256
    chunks = rows // chunk
    leaf_bits = lax.axis_size("leaf").bit_length() - 1
    sub_bits = lax.axis_size("sub").bit_length() - 1
    near_bits = leaf_bits - leaf_bits // 2
    stages = [
        Stage("leaf", 0, near_bits, 0),
        Stage("leaf", near_bits, leaf_bits - near_bits, near_bits),
        Stage("sub", 0, sub_bits, leaf_bits),
    ]
    share = rows >> near_bits
    whole = lambda a: pl.BlockSpec(
        a.shape, lambda step: (0,) * len(a.shape), pipeline_mode=pl.Buffered(1)
    )
    fixed = lambda shape: pl.BlockSpec(shape, lambda step: (0,) * len(shape))
    far = pl.BlockSpec(memory_space=pl.ANY)
    scratch = []
    for stage in stages:
        scratch += stage.scratch(share, rank)
    shape = jax.ShapeDtypeStruct
    return pl.pallas_call(
        lambda *refs: own_kernel(stages, *refs),
        grid=(2 * chunks + points // (2 * SUB),),
        in_specs=[
            pl.BlockSpec((chunk * tiles, LANES), lambda step: (jnp.minimum(step, chunks - 1), 0))
        ]
        + [whole(a) for a in (order, jitter, bases, transfer, coupling)],
        out_specs=[
            pl.BlockSpec((rows, 2 * SUB), lambda step: (0, jnp.maximum(step - 2 * chunks, 0))),
            fixed((FEATS, points)),
            fixed((rows, rank)),
            far,
            far,
        ],
        out_shape=[
            shape((rows, points), F32),
            shape((FEATS, points), BF),
            shape((rows, rank), F32),
            shape((rows + PAD, strip), F32),
            shape((rows + PAD, strip), F32),
        ],
        scratch_shapes=[
            pltpu.VMEM((points, points), BF),
            pltpu.VMEM((points, 2 * strip), F8),
            pltpu.VMEM((points, 2 * rank), BF),
            pltpu.VMEM((2 * rank + FEATS, points), BF),
            pltpu.VMEM((FEATS, points), F32),
            pltpu.VMEM((FEATS, points), F32),
            pltpu.VMEM((points, FEATS), BF),
            pltpu.VMEM((FEATS, points), BF),
            pltpu.VMEM((rows, points), BF),
            pltpu.VMEM((rows, points), F8),
            pltpu.VMEM((rows, points), F8),
            pltpu.VMEM((rows, LANES), F32),
            pltpu.VMEM((rows + PAD, strip), F32),
            pltpu.VMEM((rows + PAD, strip), F32),
            pltpu.VMEM((1 << near_bits, share // 2, 2 * rank), F32),
            pltpu.SemaphoreType.DMA((4, chunks + 1)),
        ]
        + weight_scratch(points)
        + scratch,
        compiler_params=pltpu.CompilerParams(
            vmem_limit_bytes=LIMIT, collective_id=0, has_side_effects=True
        ),
        cost_estimate=pl.CostEstimate(
            flops=31_000_000_000, bytes_accessed=30_000_000, transcendentals=4_000_000
        ),
        name="own_near",
    )(charges, order, jitter, bases, transfer, coupling)


def rest_kernel(
    factor, left_ref, right_ref, edge_ref, target_ref, expansion_ref, bases_ref, near_ref,
    out_ref, qh, q8h, q8l, units, far, basis, source_rows, source, w, w8h, w8l,
):
    strip = left_ref.shape[1]
    rank = expansion_ref.shape[1]
    row_count = near_ref.shape[0]

    @pl.when(pl.program_id(0) == 0)
    def _():
        for ref, shift, columns in (
            (left_ref, -1.0, slice(0, strip)),
            (right_ref, 1.0, slice(strip, 2 * strip)),
        ):
            coords = [ref[row_count + axis : row_count + axis + 1, :] for axis in range(3)]
            coords[0] = coords[0] + shift / GAIN
            features(coords, source_rows, None, columns)
        source[...] = jnp.transpose(source_rows[...]).astype(BF)

        @pl.loop(0, row_count // SUB)
        def _(step):
            rows = pl.ds(pl.multiple_of(step * SUB, SUB), SUB)
            joined = jnp.concatenate(
                [left_ref[rows, :] * edge_ref[0:1, 0:1], right_ref[rows, :] * edge_ref[1:2, 0:1]],
                axis=1,
            )
            full, high, rest, unit = scaled(joined)
            qh[rows, :] = high
            q8h[rows, :] = full.astype(F8)
            q8l[rows, :] = rest.astype(F8)
            units[rows, :] = jnp.broadcast_to(unit, (SUB, units.shape[1]))
            top, low = split(expansion_ref[rows, :])
            far[rows, :rank] = top
            far[rows, rank : 2 * rank] = low.astype(BF)
            far[rows, 2 * rank :] = top

        top, low = split(bases_ref[...])
        basis[:rank, :] = top
        basis[rank : 2 * rank, :] = top
        basis[2 * rank :, :] = low.astype(BF)

    def emit(rows, block, slot):
        total = mm(qh[rows, :], w[slot])
        total = total + mm(q8h[rows, :], w8l[slot])
        total = total + mm(q8l[rows, :], w8h[slot])
        inner = slice(block * SUB, (block + 1) * SUB)
        total = total * units[rows, 0:1] + near_ref[rows, inner]
        columns = pl.ds(
            pl.multiple_of((pl.program_id(0) * OUT_BLOCKS + block) * SUB, SUB), SUB
        )
        total = total * factor + mm(far[rows, :], basis[:, columns])
        first = rows.start * PAD
        for part in range(SUB // LANES):
            place = first + block * (SUB // LANES) + part
            out_ref[pl.ds(place, rows.stop - rows.start, stride=PAD), :] = total[
                :, part * LANES : (part + 1) * LANES
            ]

    sweep(source, target_ref, row_count, w, w8h, w8l, emit, OUT_BLOCKS, pl.program_id(0))


def finish(left, right, edge, target, expansion, bases, near, factor):
    rows, points = near.shape
    strip = left.shape[1]
    rank = bases.shape[0]
    width = OUT_BLOCKS * SUB
    whole = lambda a: pl.BlockSpec(a.shape, lambda step: (0, 0), pipeline_mode=pl.Buffered(1))

    def kernel(*refs):
        out = refs[7]
        flat = out.reshape(rows * PAD, LANES)
        rest_kernel(factor, *refs[:7], flat, *refs[8:])

    return pl.pallas_call(
        kernel,
        grid=(points // width,),
        in_specs=[whole(a) for a in (left, right, edge, target, expansion, bases)]
        + [pl.BlockSpec((rows, width), lambda step: (0, step))],
        out_specs=pl.BlockSpec((rows, 1, PAD, LANES), lambda step: (0, step, 0, 0)),
        out_shape=jax.ShapeDtypeStruct((rows, points // width, PAD, LANES), F32),
        scratch_shapes=[
            pltpu.VMEM((rows, 2 * strip), BF),
            pltpu.VMEM((rows, 2 * strip), F8),
            pltpu.VMEM((rows, 2 * strip), F8),
            pltpu.VMEM((rows, LANES), F32),
            pltpu.VMEM((rows, 3 * rank), BF),
            pltpu.VMEM((3 * rank, points), BF),
            pltpu.VMEM((FEATS, 2 * strip), F32),
            pltpu.VMEM((2 * strip, FEATS), BF),
        ]
        + weight_scratch(2 * strip),
        compiler_params=pltpu.CompilerParams(vmem_limit_bytes=LIMIT),
        cost_estimate=pl.CostEstimate(
            flops=10_000_000_000, bytes_accessed=21_000_000, transcendentals=2_000_000
        ),
        name="finish",
    )(left, right, edge, target, expansion, bases, near)


def body(charges, ordering, jitter, leaf_bases, transfer, coupling):
    set_count, vector_count = (charges.shape[0], charges.shape[1])
    points = charges.shape[4]
    row_count = set_count * vector_count
    near_scale = points ** (-0.5)
    leaf_basis = leaf_bases.reshape(leaf_bases.shape[2], points)
    near_part, target_rows, expansion, left, right = own_near(
        charges.reshape(row_count * (points // LANES), LANES),
        ordering.reshape(1, points),
        jitter.reshape(3, 1, points),
        leaf_basis,
        transfer,
        coupling,
    )
    position = lax.axis_index("leaf")
    inner = jnp.stack([position > 0, position < lax.axis_size("leaf") - 1])
    edge = jnp.broadcast_to(inner[:, None].astype(F32), (2, LANES))
    potential = finish(
        left, right, edge, target_rows, expansion, leaf_basis, near_part, near_scale / GAIN
    )
    return potential.reshape(set_count, vector_count, 1, 1, points)


def solution(mesh):
    in_specs = (
        P(None, None, "sub", "leaf", None),
        P("sub", "leaf", None),
        P(None, "sub", "leaf", None),
        P("sub", "leaf", None, None),
        P(),
        P(),
    )
    out_specs = P(None, None, "sub", "leaf", None)
    return jax.shard_map(body, mesh=mesh, in_specs=in_specs, out_specs=out_specs, check_vma=False)
```

```python
import jax
import jax.numpy as jnp
from jax import lax
from jax.experimental import pallas as pl
from jax.experimental.pallas import tpu as pltpu
from jax.sharding import PartitionSpec as P

DELTA_SQ = 0.0025
F8 = jnp.float8_e4m3fn
BF = jnp.bfloat16
F32 = jnp.float32
GAIN = 16.0
TOP = 384.0
FEATS = 32
SUB = 256
OUT_BLOCKS = 4
LANES = 128
PAD = 8
LIMIT = 60 * 1024 * 1024


def mm(left, right):
    return jnp.dot(left, right, preferred_element_type=F32)


def mm_nt(left, right):
    return lax.dot_general(left, right, (((1,), (1,)), ((), ())), preferred_element_type=F32)


def split(value):
    high = value.astype(BF)
    return high, value - high.astype(F32)


def features(coords, source_ref, target_ref, columns):
    ones = jnp.ones_like(coords[0])
    norm = sum(coord * coord for coord in coords)

    def pieces(value):
        out = []
        for _ in range(3):
            high, value = split(value)
            out.append(high.astype(F32))
        return out

    source = []
    target = []
    for coord in coords:
        part = pieces(coord)
        for left, right in ((0, 0), (0, 1), (1, 0), (1, 1), (0, 2), (2, 0)):
            source.append(part[left])
            target.append(-2.0 * part[right])
    source += pieces(norm + DELTA_SQ / (GAIN * GAIN)) + [ones] * 3
    target += [ones] * 3 + pieces(norm)
    blank = [jnp.zeros_like(norm)] * (FEATS - len(source))
    for ref, rows in ((source_ref, source + blank), (target_ref, target + blank)):
        if ref is not None:
            for index, row in enumerate(rows):
                ref[index : index + 1, columns] = row


def scaled(rows):
    top = jnp.maximum(jnp.max(jnp.abs(rows), axis=1, keepdims=True), 1e-30)
    full = rows * (TOP / top)
    high = full.astype(BF)
    return full, high, full - high.astype(F32), top * (1.0 / TOP)


def weigh(source_ref, target, first, last, slot, w, w8h, w8l):
    for row in range(first, last, 128):
        rows = slice(row, row + 128)
        weight = lax.rsqrt(mm(source_ref[rows, :], target))
        high = weight.astype(BF)
        w[slot, rows, :] = high
        w8h[slot, rows, :] = weight.astype(F8)
        w8l[slot, rows, :] = (weight - high.astype(F32)).astype(F8)


def sweep(source_ref, target_ref, row_count, w, w8h, w8l, emit, count, step):
    points = source_ref.shape[0]
    blocks = target_ref.shape[1] // SUB
    parts = 4

    def target(block):
        return target_ref[:, pl.ds(pl.multiple_of(block * SUB, SUB), SUB)]

    @pl.when(step == 0)
    def _():
        weigh(source_ref, target(0), 0, points, 0, w, w8h, w8l)

    height = row_count // parts
    for block in range(count):
        slot = block % 2
        coming = target(jnp.minimum(count * step + block + 1, blocks - 1))
        for part in range(parts):
            weigh(
                source_ref,
                coming,
                part * points // parts,
                (part + 1) * points // parts,
                1 - slot,
                w,
                w8h,
                w8l,
            )
            emit(slice(part * height, (part + 1) * height), block, slot)


def fine(left, right, product):
    left_high, left_low = split(left)
    right_high, right_low = split(right)
    low = product(left_low.astype(BF), right_high) + product(left_high, right_low.astype(BF))
    return product(left_high, right_high) + low


def pack(value):
    half = value.shape[0] // 2
    return jnp.concatenate([value[:half], value[half:]], axis=1)


def unpack(value):
    half = value.shape[1] // 2
    return jnp.concatenate([value[:, :half], value[:, half:]], axis=0)


class Stage:
    def __init__(self, axis, shift, bits, level):
        self.axis = axis
        self.shift = shift
        self.bits = bits
        self.level = level
        self.size = 1 << bits

    def scratch(self, share, rank):
        width = (share // 2, 2 * rank)
        count = self.size - 1
        return [
            pltpu.VMEM((self.size,) + width, F32),
            pltpu.VMEM((max(self.size - 2, 1), share, rank), F32),
            pltpu.VMEM((self.size,) + width, F32),
            pltpu.VMEM((self.size,) + width, F32),
            pltpu.VMEM(width, F32),
        ] + [pltpu.SemaphoreType.DMA((count,))] * 4

    def bind(self, refs):
        self.gathered, self.middle, self.outgoing, self.returned, self.top = refs[:5]
        self.semaphores = refs[5:]

    def member(self):
        return lax.rem(lax.axis_index(self.axis) // (1 << self.shift), self.size)

    def partner(self, offset):
        position = lax.axis_index(self.axis)
        peer = lax.rem(self.member() + offset, self.size)
        return peer, {self.axis: position + (peer - self.member()) * (1 << self.shift)}

    def copies(self, source, target, sems):
        out = []
        for offset in range(1, self.size):
            peer, device = self.partner(offset)
            out.append(
                pltpu.make_async_remote_copy(
                    src_ref=source.at[peer] if len(source.shape) == 3 else source,
                    dst_ref=target.at[self.member()],
                    send_sem=self.semaphores[sems].at[offset - 1],
                    recv_sem=self.semaphores[sems + 1].at[offset - 1],
                    device_id=device,
                    device_id_type=pl.DeviceIdType.MESH,
                )
            )
        return out

    def upward(self, source):
        return self.copies(source, self.gathered, 0)

    def downward(self):
        return self.copies(self.outgoing, self.returned, 2)

    def send_up(self, source):
        for copy in self.upward(source):
            copy.start()
        member = self.member()
        self.gathered[member] = source[member] if len(source.shape) == 3 else source[...]

    def send_down(self):
        for copy in self.downward():
            copy.start()
        member = self.member()
        self.returned[member] = self.outgoing[member]

    def levels(self, source, transfer_ref, last):
        for copy in self.upward(source):
            copy.wait_recv()
        share = self.middle.shape[1]
        nodes = [unpack(self.gathered[index]) for index in range(self.size)]
        first = 0
        for step in range(self.bits - 1 if last else self.bits):
            level = self.level + step
            even = jnp.concatenate(nodes[0::2], axis=0)
            odd = jnp.concatenate(nodes[1::2], axis=0)
            parents = fine(even, transfer_ref[level, 0], mm) + fine(odd, transfer_ref[level, 1], mm)
            nodes = [
                parents[index * share : (index + 1) * share] for index in range(len(nodes) // 2)
            ]
            if step < self.bits - 1:
                for index, value in enumerate(nodes):
                    self.middle[first + index] = value
                first += len(nodes)
            else:
                self.top[...] = pack(nodes[0])

    def expand(self, parent, transfer_ref, coupling_ref):
        share = self.middle.shape[1]
        expansions = [parent]
        starts = [0]
        for step in range(1, self.bits):
            starts.append(starts[-1] + (self.size >> step))
        for step in reversed(range(self.bits)):
            level = self.level + step
            count = self.size >> step
            if step == 0:
                held = [unpack(self.gathered[index]) for index in range(count)]
            else:
                held = [self.middle[starts[step - 1] + index] for index in range(count)]
            results = [None] * count
            for side in range(2):
                sibling = jnp.concatenate(held[1 - side :: 2], axis=0)
                value = fine(sibling, coupling_ref[level, side], mm_nt)
                if expansions[0] is not None:
                    above = jnp.concatenate(expansions, axis=0)
                    value = value + fine(above, transfer_ref[level, side], mm_nt)
                for index in range(count // 2):
                    results[2 * index + side] = value[index * share : (index + 1) * share]
            expansions = results
        for index, value in enumerate(expansions):
            self.outgoing[index] = pack(value)

    def chosen(self):
        return unpack(self.outgoing[self.member()])

    def arrived(self):
        for copy in self.downward():
            copy.wait_recv()
        return jnp.concatenate([unpack(self.returned[i]) for i in range(self.size)], axis=0)


def own_kernel(
    stages, q_ref, order_ref, jitter_ref, bases_ref, transfer_ref, coupling_ref,
    out_ref, target_out, expansion_ref, left_ref, right_ref,
    pick, pick8, basis, moved, source_rows, target_rows, feat, target, qh, q8h, q8l, unit_ref,
    tail, head, packed, edge_sems, w, w8h, w8l, *stage_refs,
):
    per_stage = len(stage_refs) // len(stages)
    for index, stage in enumerate(stages):
        stage.bind(stage_refs[index * per_stage : (index + 1) * per_stage])
    low, middle, high = stages
    points = order_ref.shape[1]
    strip = tail.shape[1]
    rank = bases_ref.shape[0]
    row_count = qh.shape[0]
    tiles = points // LANES
    chunk = q_ref.shape[0] // tiles
    chunks = row_count // chunk
    last = points - strip
    now = pl.program_id(0)
    position = lax.axis_index("leaf")
    count = lax.axis_size("leaf")
    after = {"leaf": lax.rem(position + 1, count)}
    before = {"leaf": lax.rem(position + count - 1, count)}

    def edges(first, height, slot):
        rows = pl.ds(first, height)
        return [
            pltpu.make_async_remote_copy(
                src_ref=source.at[rows, :],
                dst_ref=target.at[rows, :],
                send_sem=edge_sems.at[2 * index, slot],
                recv_sem=edge_sems.at[2 * index + 1, slot],
                device_id=device,
                device_id_type=pl.DeviceIdType.MESH,
            )
            for index, (source, target, device) in enumerate(
                ((tail, left_ref, after), (head, right_ref, before))
            )
        ]

    @pl.when(now == 0)
    def _():
        barrier = pltpu.get_barrier_semaphore()
        devices = [before, after]
        for stage in stages:
            devices += [stage.partner(offset)[1] for offset in range(1, stage.size)]
        for device in devices:
            pl.semaphore_signal(
                barrier, inc=1, device_id=device, device_id_type=pl.DeviceIdType.MESH
            )

        index = lax.broadcasted_iota(jnp.int32, (1, points), 1).astype(F32)
        coords = [(index + jitter_ref[0]) * (1.0 / points), jitter_ref[1], jitter_ref[2]]
        coords = [(coord - 0.5) * (1.0 / GAIN) for coord in coords]
        features(coords, source_rows, target_rows, slice(0, points))
        target[...] = target_rows[...].astype(BF)
        target_out[...] = target_rows[...].astype(BF)
        for axis in range(3):
            tail[row_count + axis : row_count + axis + 1, :] = coords[axis][:, last:]
            head[row_count + axis : row_count + axis + 1, :] = coords[axis][:, :strip]
        blank = jnp.zeros((PAD - 3, strip), F32)
        tail[row_count + 3 :, :] = blank
        head[row_count + 3 :, :] = blank
        top, rest = split(bases_ref[...])
        moved[:rank, :] = top
        moved[rank : 2 * rank, :] = rest.astype(BF)
        moved[2 * rank :, :] = source_rows[...].astype(BF)

        @pl.loop(0, points // SUB)
        def _(step):
            rows = pl.ds(pl.multiple_of(step * SUB, SUB), SUB)
            own = lax.broadcasted_iota(jnp.int32, (SUB, strip), 0) + step * SUB
            for part in range(points // strip):
                columns = slice(part * strip, (part + 1) * strip)
                hit = jnp.where(own == order_ref[:, columns], 1.0, 0.0)
                pick[rows, columns] = hit.astype(BF)
                if part == 0:
                    pick8[rows, :strip] = hit.astype(F8)
                if part == points // strip - 1:
                    pick8[rows, strip:] = hit.astype(F8)
            placed = mm_nt(pick[rows, :], moved[...]).astype(BF)
            feat[rows, :] = placed[:, 2 * rank :]
            basis[rows, :] = placed[:, : 2 * rank]

        pl.semaphore_wait(barrier, len(devices))

    @pl.when(now < chunks)
    def _():
        rows = pl.ds(pl.multiple_of(now * chunk, chunk), chunk)
        block = [q_ref[pl.ds(tile, chunk, stride=tiles), :] for tile in range(tiles)]
        full, top, rest, unit = scaled(jnp.concatenate(block, axis=1))
        qh[rows, :] = top
        q8h[rows, :] = full.astype(F8)
        q8l[rows, :] = rest.astype(F8)
        unit_ref[rows, :] = jnp.broadcast_to(unit, (chunk, LANES))
        both = mm(top, basis[...])
        moment = (both[:, :rank] + both[:, rank:] + mm(rest.astype(BF), basis[:, :rank])) * unit
        share = row_count // low.size
        for part in range(chunk // share):
            packed[now * (chunk // share) + part] = pack(moment[part * share : (part + 1) * share])

    @pl.when(now == chunks)
    def _():
        low.send_up(packed)

    @pl.when(jnp.logical_and(now >= chunks, now < 2 * chunks))
    def _():
        part = now - chunks
        first = pl.multiple_of(part * chunk, chunk)
        rows = pl.ds(first, chunk)
        unit = unit_ref[rows, 0:1]
        for target, picked, picked8 in (
            (tail, slice(last, points), slice(strip, 2 * strip)),
            (head, slice(0, strip), slice(0, strip)),
        ):
            target[rows, :] = (
                mm(qh[rows, :], pick[:, picked]) + mm(q8l[rows, :], pick8[:, picked8])
            ) * unit

    @pl.when(now == chunks + 1)
    def _():
        low.levels(packed, transfer_ref, False)
        middle.send_up(low.top)
        for copy in edges(row_count, PAD, chunks):
            copy.start()
        for part in range(2):
            for copy in edges(part * chunk, chunk, part):
                copy.start()

    @pl.when(now == 2 * chunks - 1)
    def _():
        middle.levels(low.top, transfer_ref, False)
        high.send_up(middle.top)

    def emit(rows, block, slot):
        total = mm(qh[rows, :], w[slot])
        total = total + mm(q8h[rows, :], w8l[slot])
        total = total + mm(q8l[rows, :], w8h[slot])
        out_ref[rows, block * SUB : (block + 1) * SUB] = total * unit_ref[rows, 0:1]

    @pl.when(now >= 2 * chunks)
    def _():
        sweep(feat, target, row_count, w, w8h, w8l, emit, 2, now - 2 * chunks)

    @pl.when(now == 2 * chunks)
    def _():
        high.levels(middle.top, transfer_ref, True)
        high.expand(None, transfer_ref, coupling_ref)
        middle.expand(high.chosen(), transfer_ref, coupling_ref)
        low.expand(middle.chosen(), transfer_ref, coupling_ref)
        low.send_down()
        for part in range(2, chunks):
            for copy in edges(part * chunk, chunk, part):
                copy.start()

    @pl.when(now == pl.num_programs(0) - 1)
    def _():
        expansion_ref[...] = low.arrived()
        for copy in low.upward(packed) + low.downward():
            copy.wait_send()
        for copy in middle.upward(low.top) + high.upward(middle.top):
            copy.wait_send()
        for part in range(chunks):
            for copy in edges(part * chunk, chunk, part):
                copy.wait()
        for copy in edges(row_count, PAD, chunks):
            copy.wait()


def weight_scratch(count):
    return [
        pltpu.VMEM((2, count, SUB), BF),
        pltpu.VMEM((2, count, SUB), F8),
        pltpu.VMEM((2, count, SUB), F8),
    ]


def own_near(charges, order, jitter, bases, transfer, coupling):
    points = order.shape[1]
    tiles = points // LANES
    rows = charges.shape[0] // tiles
    strip = points // 4
    rank = bases.shape[0]
    chunk = 256
    chunks = rows // chunk
    leaf_bits = lax.axis_size("leaf").bit_length() - 1
    sub_bits = lax.axis_size("sub").bit_length() - 1
    near_bits = leaf_bits - leaf_bits // 2
    stages = [
        Stage("leaf", 0, near_bits, 0),
        Stage("leaf", near_bits, leaf_bits - near_bits, near_bits),
        Stage("sub", 0, sub_bits, leaf_bits),
    ]
    share = rows >> near_bits
    whole = lambda a: pl.BlockSpec(
        a.shape, lambda step: (0,) * len(a.shape), pipeline_mode=pl.Buffered(1)
    )
    fixed = lambda shape: pl.BlockSpec(shape, lambda step: (0,) * len(shape))
    far = pl.BlockSpec(memory_space=pl.ANY)
    scratch = []
    for stage in stages:
        scratch += stage.scratch(share, rank)
    shape = jax.ShapeDtypeStruct
    return pl.pallas_call(
        lambda *refs: own_kernel(stages, *refs),
        grid=(2 * chunks + points // (2 * SUB),),
        in_specs=[
            pl.BlockSpec((chunk * tiles, LANES), lambda step: (jnp.minimum(step, chunks - 1), 0))
        ]
        + [whole(a) for a in (order, jitter, bases, transfer, coupling)],
        out_specs=[
            pl.BlockSpec((rows, 2 * SUB), lambda step: (0, jnp.maximum(step - 2 * chunks, 0))),
            fixed((FEATS, points)),
            fixed((rows, rank)),
            far,
            far,
        ],
        out_shape=[
            shape((rows, points), F32),
            shape((FEATS, points), BF),
            shape((rows, rank), F32),
            shape((rows + PAD, strip), F32),
            shape((rows + PAD, strip), F32),
        ],
        scratch_shapes=[
            pltpu.VMEM((points, points), BF),
            pltpu.VMEM((points, 2 * strip), F8),
            pltpu.VMEM((points, 2 * rank), BF),
            pltpu.VMEM((2 * rank + FEATS, points), BF),
            pltpu.VMEM((FEATS, points), F32),
            pltpu.VMEM((FEATS, points), F32),
            pltpu.VMEM((points, FEATS), BF),
            pltpu.VMEM((FEATS, points), BF),
            pltpu.VMEM((rows, points), BF),
            pltpu.VMEM((rows, points), F8),
            pltpu.VMEM((rows, points), F8),
            pltpu.VMEM((rows, LANES), F32),
            pltpu.VMEM((rows + PAD, strip), F32),
            pltpu.VMEM((rows + PAD, strip), F32),
            pltpu.VMEM((1 << near_bits, share // 2, 2 * rank), F32),
            pltpu.SemaphoreType.DMA((4, chunks + 1)),
        ]
        + weight_scratch(points)
        + scratch,
        compiler_params=pltpu.CompilerParams(
            vmem_limit_bytes=LIMIT, collective_id=0, has_side_effects=True
        ),
        cost_estimate=pl.CostEstimate(
            flops=31_000_000_000, bytes_accessed=30_000_000, transcendentals=4_000_000
        ),
        name="own_near",
    )(charges, order, jitter, bases, transfer, coupling)


def rest_kernel(
    factor, left_ref, right_ref, edge_ref, target_ref, expansion_ref, bases_ref, near_ref,
    out_ref, qh, q8h, q8l, units, far, basis, source_rows, source, w, w8h, w8l,
):
    strip = left_ref.shape[1]
    rank = expansion_ref.shape[1]
    row_count = near_ref.shape[0]

    @pl.when(pl.program_id(0) == 0)
    def _():
        for ref, shift, columns in (
            (left_ref, -1.0, slice(0, strip)),
            (right_ref, 1.0, slice(strip, 2 * strip)),
        ):
            coords = [ref[row_count + axis : row_count + axis + 1, :] for axis in range(3)]
            coords[0] = coords[0] + shift / GAIN
            features(coords, source_rows, None, columns)
        source[...] = jnp.transpose(source_rows[...]).astype(BF)

        @pl.loop(0, row_count // SUB)
        def _(step):
            rows = pl.ds(pl.multiple_of(step * SUB, SUB), SUB)
            joined = jnp.concatenate(
                [left_ref[rows, :] * edge_ref[0:1, 0:1], right_ref[rows, :] * edge_ref[1:2, 0:1]],
                axis=1,
            )
            full, high, rest, unit = scaled(joined)
            qh[rows, :] = high
            q8h[rows, :] = full.astype(F8)
            q8l[rows, :] = rest.astype(F8)
            units[rows, :] = jnp.broadcast_to(unit, (SUB, units.shape[1]))
            top, low = split(expansion_ref[rows, :])
            far[rows, :rank] = top
            far[rows, rank : 2 * rank] = low.astype(BF)
            far[rows, 2 * rank :] = top

        top, low = split(bases_ref[...])
        basis[:rank, :] = top
        basis[rank : 2 * rank, :] = top
        basis[2 * rank :, :] = low.astype(BF)

    def emit(rows, block, slot):
        total = mm(qh[rows, :], w[slot])
        total = total + mm(q8h[rows, :], w8l[slot])
        total = total + mm(q8l[rows, :], w8h[slot])
        inner = slice(block * SUB, (block + 1) * SUB)
        total = total * units[rows, 0:1] + near_ref[rows, inner]
        columns = pl.ds(
            pl.multiple_of((pl.program_id(0) * OUT_BLOCKS + block) * SUB, SUB), SUB
        )
        total = total * factor + mm(far[rows, :], basis[:, columns])
        first = rows.start * PAD
        for part in range(SUB // LANES):
            place = first + block * (SUB // LANES) + part
            out_ref[pl.ds(place, rows.stop - rows.start, stride=PAD), :] = total[
                :, part * LANES : (part + 1) * LANES
            ]

    sweep(source, target_ref, row_count, w, w8h, w8l, emit, OUT_BLOCKS, pl.program_id(0))


def finish(left, right, edge, target, expansion, bases, near, factor):
    rows, points = near.shape
    strip = left.shape[1]
    rank = bases.shape[0]
    width = OUT_BLOCKS * SUB
    whole = lambda a: pl.BlockSpec(a.shape, lambda step: (0, 0), pipeline_mode=pl.Buffered(1))

    def kernel(*refs):
        out = refs[7]
        flat = out.reshape(rows * PAD, LANES)
        rest_kernel(factor, *refs[:7], flat, *refs[8:])

    return pl.pallas_call(
        kernel,
        grid=(points // width,),
        in_specs=[whole(a) for a in (left, right, edge, target, expansion, bases)]
        + [pl.BlockSpec((rows, width), lambda step: (0, step))],
        out_specs=pl.BlockSpec((rows, 1, PAD, LANES), lambda step: (0, step, 0, 0)),
        out_shape=jax.ShapeDtypeStruct((rows, points // width, PAD, LANES), F32),
        scratch_shapes=[
            pltpu.VMEM((rows, 2 * strip), BF),
            pltpu.VMEM((rows, 2 * strip), F8),
            pltpu.VMEM((rows, 2 * strip), F8),
            pltpu.VMEM((rows, LANES), F32),
            pltpu.VMEM((rows, 3 * rank), BF),
            pltpu.VMEM((3 * rank, points), BF),
            pltpu.VMEM((FEATS, 2 * strip), F32),
            pltpu.VMEM((2 * strip, FEATS), BF),
        ]
        + weight_scratch(2 * strip),
        compiler_params=pltpu.CompilerParams(vmem_limit_bytes=LIMIT),
        cost_estimate=pl.CostEstimate(
            flops=10_000_000_000, bytes_accessed=21_000_000, transcendentals=2_000_000
        ),
        name="finish",
    )(left, right, edge, target, expansion, bases, near)


def body(charges, ordering, jitter, leaf_bases, transfer, coupling):
    set_count, vector_count = (charges.shape[0], charges.shape[1])
    points = charges.shape[4]
    row_count = set_count * vector_count
    near_scale = points ** (-0.5)
    leaf_basis = leaf_bases.reshape(leaf_bases.shape[2], points)
    near_part, target_rows, expansion, left, right = own_near(
        charges.reshape(row_count * (points // LANES), LANES),
        ordering.reshape(1, points),
        jitter.reshape(3, 1, points),
        leaf_basis,
        transfer,
        coupling,
    )
    position = lax.axis_index("leaf")
    inner = jnp.stack([position > 0, position < lax.axis_size("leaf") - 1])
    edge = jnp.broadcast_to(inner[:, None].astype(F32), (2, LANES))
    potential = finish(
        left, right, edge, target_rows, expansion, leaf_basis, near_part, near_scale / GAIN
    )
    return potential.reshape(set_count, vector_count, 1, 1, points)


def solution(mesh):
    in_specs = (
        P(None, None, "sub", "leaf", None),
        P("sub", "leaf", None),
        P(None, "sub", "leaf", None),
        P("sub", "leaf", None, None),
        P(),
        P(),
    )
    out_specs = P(None, None, "sub", "leaf", None)
    return jax.shard_map(body, mesh=mesh, in_specs=in_specs, out_specs=out_specs, check_vma=False)
```

```python
import jax
import jax.numpy as jnp
from jax import lax
from jax.experimental import pallas as pl
from jax.experimental.pallas import tpu as pltpu
from jax.sharding import PartitionSpec as P

DELTA_SQ = 0.0025
F8 = jnp.float8_e4m3fn
BF = jnp.bfloat16
F32 = jnp.float32
GAIN = 16.0
TOP = 384.0
FEATS = 32
SUB = 256
OUT_BLOCKS = 4
LANES = 128
PAD = 8
LIMIT = 60 * 1024 * 1024


def mm(left, right):
    return jnp.dot(left, right, preferred_element_type=F32)


def mm_nt(left, right):
    return lax.dot_general(left, right, (((1,), (1,)), ((), ())), preferred_element_type=F32)


def split(value):
    high = value.astype(BF)
    return high, value - high.astype(F32)


def features(coords, source_ref, target_ref, columns):
    ones = jnp.ones_like(coords[0])
    norm = sum(coord * coord for coord in coords)

    def pieces(value):
        out = []
        for _ in range(3):
            high, value = split(value)
            out.append(high.astype(F32))
        return out

    source = []
    target = []
    for coord in coords:
        part = pieces(coord)
        for left, right in ((0, 0), (0, 1), (1, 0), (1, 1), (0, 2), (2, 0)):
            source.append(part[left])
            target.append(-2.0 * part[right])
    source += pieces(norm + DELTA_SQ / (GAIN * GAIN)) + [ones] * 3
    target += [ones] * 3 + pieces(norm)
    blank = [jnp.zeros_like(norm)] * (FEATS - len(source))
    for ref, rows in ((source_ref, source + blank), (target_ref, target + blank)):
        if ref is not None:
            for index, row in enumerate(rows):
                ref[index : index + 1, columns] = row


def scaled(rows):
    top = jnp.maximum(jnp.max(jnp.abs(rows), axis=1, keepdims=True), 1e-30)
    full = rows * (TOP / top)
    high = full.astype(BF)
    return full, high, full - high.astype(F32), top * (1.0 / TOP)


def weigh(source_ref, target, first, last, slot, w, w8h, w8l):
    for row in range(first, last, 128):
        rows = slice(row, row + 128)
        weight = lax.rsqrt(mm(source_ref[rows, :], target))
        high = weight.astype(BF)
        w[slot, rows, :] = high
        w8h[slot, rows, :] = weight.astype(F8)
        w8l[slot, rows, :] = (weight - high.astype(F32)).astype(F8)


def sweep(source_ref, target_ref, row_count, w, w8h, w8l, emit, count, step):
    points = source_ref.shape[0]
    blocks = target_ref.shape[1] // SUB
    parts = 4

    def target(block):
        return target_ref[:, pl.ds(pl.multiple_of(block * SUB, SUB), SUB)]

    @pl.when(step == 0)
    def _():
        weigh(source_ref, target(0), 0, points, 0, w, w8h, w8l)

    height = row_count // parts
    for block in range(count):
        slot = block % 2
        coming = target(jnp.minimum(count * step + block + 1, blocks - 1))
        for part in range(parts):
            weigh(
                source_ref,
                coming,
                part * points // parts,
                (part + 1) * points // parts,
                1 - slot,
                w,
                w8h,
                w8l,
            )
            emit(slice(part * height, (part + 1) * height), block, slot)


def fine(left, right, product):
    left_high, left_low = split(left)
    right_high, right_low = split(right)
    low = product(left_low.astype(BF), right_high) + product(left_high, right_low.astype(BF))
    return product(left_high, right_high) + low


def pack(value):
    half = value.shape[0] // 2
    return jnp.concatenate([value[:half], value[half:]], axis=1)


def unpack(value):
    half = value.shape[1] // 2
    return jnp.concatenate([value[:, :half], value[:, half:]], axis=0)


class Stage:
    def __init__(self, axis, shift, bits, level):
        self.axis = axis
        self.shift = shift
        self.bits = bits
        self.level = level
        self.size = 1 << bits

    def scratch(self, share, rank):
        width = (share // 2, 2 * rank)
        count = self.size - 1
        return [
            pltpu.VMEM((self.size,) + width, F32),
            pltpu.VMEM((max(self.size - 2, 1), share, rank), F32),
            pltpu.VMEM((self.size,) + width, F32),
            pltpu.VMEM((self.size,) + width, F32),
            pltpu.VMEM(width, F32),
        ] + [pltpu.SemaphoreType.DMA((count,))] * 4

    def bind(self, refs):
        self.gathered, self.middle, self.outgoing, self.returned, self.top = refs[:5]
        self.semaphores = refs[5:]

    def member(self):
        return lax.rem(lax.axis_index(self.axis) // (1 << self.shift), self.size)

    def partner(self, offset):
        position = lax.axis_index(self.axis)
        peer = lax.rem(self.member() + offset, self.size)
        return peer, {self.axis: position + (peer - self.member()) * (1 << self.shift)}

    def copies(self, source, target, sems):
        out = []
        for offset in range(1, self.size):
            peer, device = self.partner(offset)
            out.append(
                pltpu.make_async_remote_copy(
                    src_ref=source.at[peer] if len(source.shape) == 3 else source,
                    dst_ref=target.at[self.member()],
                    send_sem=self.semaphores[sems].at[offset - 1],
                    recv_sem=self.semaphores[sems + 1].at[offset - 1],
                    device_id=device,
                    device_id_type=pl.DeviceIdType.MESH,
                )
            )
        return out

    def upward(self, source):
        return self.copies(source, self.gathered, 0)

    def downward(self):
        return self.copies(self.outgoing, self.returned, 2)

    def send_up(self, source):
        for copy in self.upward(source):
            copy.start()
        member = self.member()
        self.gathered[member] = source[member] if len(source.shape) == 3 else source[...]

    def send_down(self):
        for copy in self.downward():
            copy.start()
        member = self.member()
        self.returned[member] = self.outgoing[member]

    def levels(self, source, transfer_ref, last):
        for copy in self.upward(source):
            copy.wait_recv()
        share = self.middle.shape[1]
        nodes = [unpack(self.gathered[index]) for index in range(self.size)]
        first = 0
        for step in range(self.bits - 1 if last else self.bits):
            level = self.level + step
            even = jnp.concatenate(nodes[0::2], axis=0)
            odd = jnp.concatenate(nodes[1::2], axis=0)
            parents = fine(even, transfer_ref[level, 0], mm) + fine(odd, transfer_ref[level, 1], mm)
            nodes = [
                parents[index * share : (index + 1) * share] for index in range(len(nodes) // 2)
            ]
            if step < self.bits - 1:
                for index, value in enumerate(nodes):
                    self.middle[first + index] = value
                first += len(nodes)
            else:
                self.top[...] = pack(nodes[0])

    def expand(self, parent, transfer_ref, coupling_ref):
        share = self.middle.shape[1]
        expansions = [parent]
        starts = [0]
        for step in range(1, self.bits):
            starts.append(starts[-1] + (self.size >> step))
        for step in reversed(range(self.bits)):
            level = self.level + step
            count = self.size >> step
            if step == 0:
                held = [unpack(self.gathered[index]) for index in range(count)]
            else:
                held = [self.middle[starts[step - 1] + index] for index in range(count)]
            results = [None] * count
            for side in range(2):
                sibling = jnp.concatenate(held[1 - side :: 2], axis=0)
                value = fine(sibling, coupling_ref[level, side], mm_nt)
                if expansions[0] is not None:
                    above = jnp.concatenate(expansions, axis=0)
                    value = value + fine(above, transfer_ref[level, side], mm_nt)
                for index in range(count // 2):
                    results[2 * index + side] = value[index * share : (index + 1) * share]
            expansions = results
        for index, value in enumerate(expansions):
            self.outgoing[index] = pack(value)

    def chosen(self):
        return unpack(self.outgoing[self.member()])

    def arrived(self):
        for copy in self.downward():
            copy.wait_recv()
        return jnp.concatenate([unpack(self.returned[i]) for i in range(self.size)], axis=0)


def own_kernel(
    stages, q_ref, order_ref, jitter_ref, bases_ref, transfer_ref, coupling_ref,
    out_ref, target_out, expansion_ref, left_ref, right_ref,
    pick, pick8, basis, moved, source_rows, target_rows, feat, target, qh, q8h, q8l, unit_ref,
    tail, head, packed, edge_sems, w, w8h, w8l, *stage_refs,
):
    per_stage = len(stage_refs) // len(stages)
    for index, stage in enumerate(stages):
        stage.bind(stage_refs[index * per_stage : (index + 1) * per_stage])
    low, middle, high = stages
    points = order_ref.shape[1]
    strip = tail.shape[1]
    rank = bases_ref.shape[0]
    row_count = qh.shape[0]
    tiles = points // LANES
    chunk = q_ref.shape[0] // tiles
    chunks = row_count // chunk
    last = points - strip
    now = pl.program_id(0)
    position = lax.axis_index("leaf")
    count = lax.axis_size("leaf")
    after = {"leaf": lax.rem(position + 1, count)}
    before = {"leaf": lax.rem(position + count - 1, count)}

    def edges(first, height, slot):
        rows = pl.ds(first, height)
        return [
            pltpu.make_async_remote_copy(
                src_ref=source.at[rows, :],
                dst_ref=target.at[rows, :],
                send_sem=edge_sems.at[2 * index, slot],
                recv_sem=edge_sems.at[2 * index + 1, slot],
                device_id=device,
                device_id_type=pl.DeviceIdType.MESH,
            )
            for index, (source, target, device) in enumerate(
                ((tail, left_ref, after), (head, right_ref, before))
            )
        ]

    @pl.when(now == 0)
    def _():
        barrier = pltpu.get_barrier_semaphore()
        devices = [before, after]
        for stage in stages:
            devices += [stage.partner(offset)[1] for offset in range(1, stage.size)]
        for device in devices:
            pl.semaphore_signal(
                barrier, inc=1, device_id=device, device_id_type=pl.DeviceIdType.MESH
            )

        index = lax.broadcasted_iota(jnp.int32, (1, points), 1).astype(F32)
        coords = [(index + jitter_ref[0]) * (1.0 / points), jitter_ref[1], jitter_ref[2]]
        coords = [(coord - 0.5) * (1.0 / GAIN) for coord in coords]
        features(coords, source_rows, target_rows, slice(0, points))
        target[...] = target_rows[...].astype(BF)
        target_out[...] = target_rows[...].astype(BF)
        for axis in range(3):
            tail[row_count + axis : row_count + axis + 1, :] = coords[axis][:, last:]
            head[row_count + axis : row_count + axis + 1, :] = coords[axis][:, :strip]
        blank = jnp.zeros((PAD - 3, strip), F32)
        tail[row_count + 3 :, :] = blank
        head[row_count + 3 :, :] = blank
        top, rest = split(bases_ref[...])
        moved[:rank, :] = top
        moved[rank : 2 * rank, :] = rest.astype(BF)
        moved[2 * rank :, :] = source_rows[...].astype(BF)

        @pl.loop(0, points // SUB)
        def _(step):
            rows = pl.ds(pl.multiple_of(step * SUB, SUB), SUB)
            own = lax.broadcasted_iota(jnp.int32, (SUB, strip), 0) + step * SUB
            for part in range(points // strip):
                columns = slice(part * strip, (part + 1) * strip)
                hit = jnp.where(own == order_ref[:, columns], 1.0, 0.0)
                pick[rows, columns] = hit.astype(BF)
                if part == 0:
                    pick8[rows, :strip] = hit.astype(F8)
                if part == points // strip - 1:
                    pick8[rows, strip:] = hit.astype(F8)
            placed = mm_nt(pick[rows, :], moved[...]).astype(BF)
            feat[rows, :] = placed[:, 2 * rank :]
            basis[rows, :] = placed[:, : 2 * rank]

        pl.semaphore_wait(barrier, len(devices))

    @pl.when(now < chunks)
    def _():
        rows = pl.ds(pl.multiple_of(now * chunk, chunk), chunk)
        block = [q_ref[pl.ds(tile, chunk, stride=tiles), :] for tile in range(tiles)]
        full, top, rest, unit = scaled(jnp.concatenate(block, axis=1))
        qh[rows, :] = top
        q8h[rows, :] = full.astype(F8)
        q8l[rows, :] = rest.astype(F8)
        unit_ref[rows, :] = jnp.broadcast_to(unit, (chunk, LANES))
        both = mm(top, basis[...])
        moment = (both[:, :rank] + both[:, rank:] + mm(rest.astype(BF), basis[:, :rank])) * unit
        share = row_count // low.size
        for part in range(chunk // share):
            packed[now * (chunk // share) + part] = pack(moment[part * share : (part + 1) * share])

    @pl.when(now == chunks)
    def _():
        low.send_up(packed)

    @pl.when(jnp.logical_and(now >= chunks, now < 2 * chunks))
    def _():
        part = now - chunks
        first = pl.multiple_of(part * chunk, chunk)
        rows = pl.ds(first, chunk)
        unit = unit_ref[rows, 0:1]
        for target, picked, picked8 in (
            (tail, slice(last, points), slice(strip, 2 * strip)),
            (head, slice(0, strip), slice(0, strip)),
        ):
            target[rows, :] = (
                mm(qh[rows, :], pick[:, picked]) + mm(q8l[rows, :], pick8[:, picked8])
            ) * unit

    @pl.when(now == chunks + 1)
    def _():
        low.levels(packed, transfer_ref, False)
        middle.send_up(low.top)
        for copy in edges(row_count, PAD, chunks):
            copy.start()
        for part in range(0, 1):
            for copy in edges(part * chunk, chunk, part):
                copy.start()

    @pl.when(now == 2 * chunks - 1)
    def _():
        middle.levels(low.top, transfer_ref, False)
        high.send_up(middle.top)
        for part in range(1, 2):
            for copy in edges(part * chunk, chunk, part):
                copy.start()

    def emit(rows, block, slot):
        total = mm(qh[rows, :], w[slot])
        total = total + mm(q8h[rows, :], w8l[slot])
        total = total + mm(q8l[rows, :], w8h[slot])
        out_ref[rows, block * SUB : (block + 1) * SUB] = total * unit_ref[rows, 0:1]

    @pl.when(now >= 2 * chunks)
    def _():
        sweep(feat, target, row_count, w, w8h, w8l, emit, 2, now - 2 * chunks)

    @pl.when(now == 2 * chunks)
    def _():
        high.levels(middle.top, transfer_ref, True)
        high.expand(None, transfer_ref, coupling_ref)
        middle.expand(high.chosen(), transfer_ref, coupling_ref)
        low.expand(middle.chosen(), transfer_ref, coupling_ref)
        low.send_down()
        for part in range(2, chunks):
            for copy in edges(part * chunk, chunk, part):
                copy.start()

    @pl.when(now == pl.num_programs(0) - 1)
    def _():
        expansion_ref[...] = low.arrived()
        for copy in low.upward(packed) + low.downward():
            copy.wait_send()
        for copy in middle.upward(low.top) + high.upward(middle.top):
            copy.wait_send()
        for part in range(chunks):
            for copy in edges(part * chunk, chunk, part):
                copy.wait()
        for copy in edges(row_count, PAD, chunks):
            copy.wait()


def weight_scratch(count):
    return [
        pltpu.VMEM((2, count, SUB), BF),
        pltpu.VMEM((2, count, SUB), F8),
        pltpu.VMEM((2, count, SUB), F8),
    ]


def own_near(charges, order, jitter, bases, transfer, coupling):
    points = order.shape[1]
    tiles = points // LANES
    rows = charges.shape[0] // tiles
    strip = points // 4
    rank = bases.shape[0]
    chunk = 256
    chunks = rows // chunk
    leaf_bits = lax.axis_size("leaf").bit_length() - 1
    sub_bits = lax.axis_size("sub").bit_length() - 1
    near_bits = leaf_bits - leaf_bits // 2
    stages = [
        Stage("leaf", 0, near_bits, 0),
        Stage("leaf", near_bits, leaf_bits - near_bits, near_bits),
        Stage("sub", 0, sub_bits, leaf_bits),
    ]
    share = rows >> near_bits
    whole = lambda a: pl.BlockSpec(
        a.shape, lambda step: (0,) * len(a.shape), pipeline_mode=pl.Buffered(1)
    )
    fixed = lambda shape: pl.BlockSpec(shape, lambda step: (0,) * len(shape))
    far = pl.BlockSpec(memory_space=pl.ANY)
    scratch = []
    for stage in stages:
        scratch += stage.scratch(share, rank)
    shape = jax.ShapeDtypeStruct
    return pl.pallas_call(
        lambda *refs: own_kernel(stages, *refs),
        grid=(2 * chunks + points // (2 * SUB),),
        in_specs=[
            pl.BlockSpec((chunk * tiles, LANES), lambda step: (jnp.minimum(step, chunks - 1), 0))
        ]
        + [whole(a) for a in (order, jitter, bases, transfer, coupling)],
        out_specs=[
            pl.BlockSpec((rows, 2 * SUB), lambda step: (0, jnp.maximum(step - 2 * chunks, 0))),
            fixed((FEATS, points)),
            fixed((rows, rank)),
            far,
            far,
        ],
        out_shape=[
            shape((rows, points), F32),
            shape((FEATS, points), BF),
            shape((rows, rank), F32),
            shape((rows + PAD, strip), F32),
            shape((rows + PAD, strip), F32),
        ],
        scratch_shapes=[
            pltpu.VMEM((points, points), BF),
            pltpu.VMEM((points, 2 * strip), F8),
            pltpu.VMEM((points, 2 * rank), BF),
            pltpu.VMEM((2 * rank + FEATS, points), BF),
            pltpu.VMEM((FEATS, points), F32),
            pltpu.VMEM((FEATS, points), F32),
            pltpu.VMEM((points, FEATS), BF),
            pltpu.VMEM((FEATS, points), BF),
            pltpu.VMEM((rows, points), BF),
            pltpu.VMEM((rows, points), F8),
            pltpu.VMEM((rows, points), F8),
            pltpu.VMEM((rows, LANES), F32),
            pltpu.VMEM((rows + PAD, strip), F32),
            pltpu.VMEM((rows + PAD, strip), F32),
            pltpu.VMEM((1 << near_bits, share // 2, 2 * rank), F32),
            pltpu.SemaphoreType.DMA((4, chunks + 1)),
        ]
        + weight_scratch(points)
        + scratch,
        compiler_params=pltpu.CompilerParams(
            vmem_limit_bytes=LIMIT, collective_id=0, has_side_effects=True
        ),
        cost_estimate=pl.CostEstimate(
            flops=31_000_000_000, bytes_accessed=30_000_000, transcendentals=4_000_000
        ),
        name="own_near",
    )(charges, order, jitter, bases, transfer, coupling)


def rest_kernel(
    factor, left_ref, right_ref, edge_ref, target_ref, expansion_ref, bases_ref, near_ref,
    out_ref, qh, q8h, q8l, units, far, basis, source_rows, source, w, w8h, w8l,
):
    strip = left_ref.shape[1]
    rank = expansion_ref.shape[1]
    row_count = near_ref.shape[0]

    @pl.when(pl.program_id(0) == 0)
    def _():
        for ref, shift, columns in (
            (left_ref, -1.0, slice(0, strip)),
            (right_ref, 1.0, slice(strip, 2 * strip)),
        ):
            coords = [ref[row_count + axis : row_count + axis + 1, :] for axis in range(3)]
            coords[0] = coords[0] + shift / GAIN
            features(coords, source_rows, None, columns)
        source[...] = jnp.transpose(source_rows[...]).astype(BF)

        @pl.loop(0, row_count // SUB)
        def _(step):
            rows = pl.ds(pl.multiple_of(step * SUB, SUB), SUB)
            joined = jnp.concatenate(
                [left_ref[rows, :] * edge_ref[0:1, 0:1], right_ref[rows, :] * edge_ref[1:2, 0:1]],
                axis=1,
            )
            full, high, rest, unit = scaled(joined)
            qh[rows, :] = high
            q8h[rows, :] = full.astype(F8)
            q8l[rows, :] = rest.astype(F8)
            units[rows, :] = jnp.broadcast_to(unit, (SUB, units.shape[1]))
            top, low = split(expansion_ref[rows, :])
            far[rows, :rank] = top
            far[rows, rank : 2 * rank] = low.astype(BF)
            far[rows, 2 * rank :] = top

        top, low = split(bases_ref[...])
        basis[:rank, :] = top
        basis[rank : 2 * rank, :] = top
        basis[2 * rank :, :] = low.astype(BF)

    def emit(rows, block, slot):
        total = mm(qh[rows, :], w[slot])
        total = total + mm(q8h[rows, :], w8l[slot])
        total = total + mm(q8l[rows, :], w8h[slot])
        inner = slice(block * SUB, (block + 1) * SUB)
        total = total * units[rows, 0:1] + near_ref[rows, inner]
        columns = pl.ds(
            pl.multiple_of((pl.program_id(0) * OUT_BLOCKS + block) * SUB, SUB), SUB
        )
        total = total * factor + mm(far[rows, :], basis[:, columns])
        first = rows.start * PAD
        for part in range(SUB // LANES):
            place = first + block * (SUB // LANES) + part
            out_ref[pl.ds(place, rows.stop - rows.start, stride=PAD), :] = total[
                :, part * LANES : (part + 1) * LANES
            ]

    sweep(source, target_ref, row_count, w, w8h, w8l, emit, OUT_BLOCKS, pl.program_id(0))


def finish(left, right, edge, target, expansion, bases, near, factor):
    rows, points = near.shape
    strip = left.shape[1]
    rank = bases.shape[0]
    width = OUT_BLOCKS * SUB
    whole = lambda a: pl.BlockSpec(a.shape, lambda step: (0, 0), pipeline_mode=pl.Buffered(1))

    def kernel(*refs):
        out = refs[7]
        flat = out.reshape(rows * PAD, LANES)
        rest_kernel(factor, *refs[:7], flat, *refs[8:])

    return pl.pallas_call(
        kernel,
        grid=(points // width,),
        in_specs=[whole(a) for a in (left, right, edge, target, expansion, bases)]
        + [pl.BlockSpec((rows, width), lambda step: (0, step))],
        out_specs=pl.BlockSpec((rows, 1, PAD, LANES), lambda step: (0, step, 0, 0)),
        out_shape=jax.ShapeDtypeStruct((rows, points // width, PAD, LANES), F32),
        scratch_shapes=[
            pltpu.VMEM((rows, 2 * strip), BF),
            pltpu.VMEM((rows, 2 * strip), F8),
            pltpu.VMEM((rows, 2 * strip), F8),
            pltpu.VMEM((rows, LANES), F32),
            pltpu.VMEM((rows, 3 * rank), BF),
            pltpu.VMEM((3 * rank, points), BF),
            pltpu.VMEM((FEATS, 2 * strip), F32),
            pltpu.VMEM((2 * strip, FEATS), BF),
        ]
        + weight_scratch(2 * strip),
        compiler_params=pltpu.CompilerParams(vmem_limit_bytes=LIMIT),
        cost_estimate=pl.CostEstimate(
            flops=10_000_000_000, bytes_accessed=21_000_000, transcendentals=2_000_000
        ),
        name="finish",
    )(left, right, edge, target, expansion, bases, near)


def body(charges, ordering, jitter, leaf_bases, transfer, coupling):
    set_count, vector_count = (charges.shape[0], charges.shape[1])
    points = charges.shape[4]
    row_count = set_count * vector_count
    near_scale = points ** (-0.5)
    leaf_basis = leaf_bases.reshape(leaf_bases.shape[2], points)
    near_part, target_rows, expansion, left, right = own_near(
        charges.reshape(row_count * (points // LANES), LANES),
        ordering.reshape(1, points),
        jitter.reshape(3, 1, points),
        leaf_basis,
        transfer,
        coupling,
    )
    position = lax.axis_index("leaf")
    inner = jnp.stack([position > 0, position < lax.axis_size("leaf") - 1])
    edge = jnp.broadcast_to(inner[:, None].astype(F32), (2, LANES))
    potential = finish(
        left, right, edge, target_rows, expansion, leaf_basis, near_part, near_scale / GAIN
    )
    return potential.reshape(set_count, vector_count, 1, 1, points)


def solution(mesh):
    in_specs = (
        P(None, None, "sub", "leaf", None),
        P("sub", "leaf", None),
        P(None, "sub", "leaf", None),
        P("sub", "leaf", None, None),
        P(),
        P(),
    )
    out_specs = P(None, None, "sub", "leaf", None)
    return jax.shard_map(body, mesh=mesh, in_specs=in_specs, out_specs=out_specs, check_vma=False)
```
